512 devices in a mesh: wide: 64 (over x, y, core), narrow: 8 (over z).
Axes of the slice: x: 4, y: 8, z: 8, core: 2. Of those that a mesh axis runs over, the one named last changes fastest.
Arguments:
- kernel: float32 [32768, 64, 128], P(('wide', 'narrow')), may hold values from 0 to 0.015625
- volume: float32 [32768, 64], P(('wide', 'narrow')), may hold values from 0.5 to 4
- velocity: float32 [32768, 3, 64], P(('wide', 'narrow')), may hold values from -6 to 6
- block_brick: int32 [32768, 1], P(('wide', 'narrow')), may hold values from 0 to 63; in each aligned block of 64 rows (0 to 63, 64 to 127, ...) at most 2 rows name the same one
- block_tile: int32 [32768], P(('wide', 'narrow')), may hold values from 0 to 127
- fluid_velocity: float32 [3, 256, 64, 512], P(None, 'wide', 'narrow'), may hold values from -6 to 6
Outputs:
- particle_drag: float32 [32768, 3, 64], P(('wide', 'narrow'))
- pressure: float32 [256, 64, 512], P('wide', 'narrow')
- fluid_next: float32 [3, 256, 64, 512], P(None, 'wide', 'narrow')
The draws below stay inside these ranges and needn't reach their ends.
Inputs may be any that keep to these rules, and one draw needn't show every extreme that they name: `block_brick`: among the 64 blocks of one device, at most 2 name the same brick, a bound that some block reaches.
All inputs are finite; a program needn't handle non-finite values.
Results may differ from the reference program's by a relative error of at most 0.00007.
Values sent between devices are 32-bit elements; how exact they have to be, the bound alone decides.
No kernel may reach another device: no remote copies, remote signals or barrier semaphores. Data moves between devices by JAX's collectives and lax.ppermute only.
A program may use at most 64 MiB of HBM per device.

```python
import math
import jax
import jax.numpy as jnp
import numpy as np
from jax import lax

PART_BLK = 64
TILE_CELLS = 128
CX = 4
CZ = 8
NY = 512
BLK_DEV = 64
SWEEPS = 6
TILES_DEV = 128
CAP = 2
BLOCKS = 32768
NX = 256
NZ = 64
N_WIDE = 64
N_NARROW = 8


def touch_ends(array, rng, smallest, high):
    longest = array.shape.index(max(array.shape))
    spots = []
    for shift in (0, 1):
        where = [jax.random.randint(jax.random.fold_in(rng, axis), (), 0, length) for axis, length in enumerate(array.shape)]
        where[longest] = (where[longest] + shift) % array.shape[longest]
        spots.append(tuple(where))
    return array.at[spots[0]].set(smallest).at[spots[1]].set(high)


def shard_levels(rng, dims, pieces, least, high):
    factor_of = 1.0
    for axis_at, shards_of in pieces:
        heights = jax.random.uniform(jax.random.fold_in(jax.random.fold_in(rng, 6), axis_at), (shards_of,), jnp.float32, least / len(pieces), high / len(pieces))
        factor_of = factor_of * jnp.repeat(jnp.exp(heights), dims[axis_at] // shards_of).reshape((-1,) + (1,) * (len(dims) - 1 - axis_at))
    return factor_of


def routed_block(key, own, number, rows, number_of, top, bound, slope):
    ranking = jax.random.permutation(key, number_of)
    heavy_load, usual = portions_of(number_of, rows * top, bound, slope, True), portions_of(number_of, rows * top, bound, slope, False)
    places = jnp.arange(number_of)

    def named(lengths, rotation):
        used = int((lengths > 0).sum())
        fixed = max(1, used // 4)
        passed = fixed + (places - fixed + rotation * (used - fixed)) % max(1, number_of - fixed)
        return jnp.zeros((number_of,), jnp.int32).at[ranking[jnp.where(places < fixed, places, passed)]].set(jnp.asarray(lengths, jnp.int32))

    lengths = jnp.where(number % 4 == 0, named(heavy_load, number // 4), named(usual, number - number // 4 - 1))
    mixed = jax.random.permutation(jax.random.fold_in(own, 3), number_of)
    giver, sink = mixed[0:number_of // 2 * 2:2], mixed[1:number_of // 2 * 2:2]
    slack = jnp.minimum(lengths[giver] - 1, bound - lengths[sink]) // 2
    slack = jnp.where((giver == ranking[0]) | (sink == ranking[0]) | (lengths[sink] == 0), 0, jnp.maximum(slack, 0))
    passed = jax.random.randint(jax.random.fold_in(own, 4), (number_of // 2,), 0, 1 << 20) % (slack + 1)
    lengths = lengths.at[giver].add(-passed).at[sink].add(passed)
    items = jnp.searchsorted(jnp.cumsum(lengths), jnp.arange(rows * top), side="right").astype(jnp.int32)
    listing = items.reshape(top, rows).T
    listing = listing[jax.random.permutation(jax.random.fold_in(own, 1), rows)]
    rotation = jax.random.randint(jax.random.fold_in(own, 2), (rows, 1), 0, top)
    return jnp.take_along_axis(listing, (jnp.arange(top)[None, :] + rotation) % top, axis=1)


def portions_of(number_of, total, reach, skew, full):
    weights = [(1 << 20) // math.isqrt(standing ** skew) + 1 for standing in range(1, number_of + 1)]
    largest = reach if full else min(reach, max(-(-total // number_of), total * weights[0] // sum(weights)))
    least = 1 if total - largest >= number_of - 1 else 0
    counts, surplus = [largest] + [least] * (number_of - 1), total - largest - least * (number_of - 1)
    while surplus > 0:
        free = [i for i in range(1, number_of) if counts[i] < largest] or [i for i in range(1, number_of) if counts[i] < reach]
        whole, left = sum([weights[i] for i in free]), surplus
        for i in free:
            addition = min(reach - counts[i], max(1, left * weights[i] // whole), surplus)
            counts[i] = counts[i] + addition
            surplus = surplus - addition
    return np.array(counts)


def gaussian(own_key, dims, deviation, bound, shards=(), held_as=jnp.bfloat16):
    array = jax.random.normal(own_key, dims, jnp.float32) * deviation
    if len(shards) > 0:
        array = shard_levels(own_key, dims, shards, -0.22, 0.18) * array
    return jnp.clip(array, min=-bound, max=bound).astype(held_as)


def setup_inputs(seed: int = 0) -> dict:
    arg_keys = jax.random.split(jax.random.key(seed), 7)
    kernel = jnp.clip(0.015625 * jax.random.uniform(arg_keys[0], (BLOCKS, PART_BLK, TILE_CELLS), jnp.float32) ** shard_levels(arg_keys[0], (BLOCKS, PART_BLK, TILE_CELLS), ((0, 512),), -0.2, 0.2), 0.0, 0.015625)
    volume = jnp.clip(jnp.exp(math.log(4.0) - 2.0794415 * jax.random.uniform(arg_keys[1], (BLOCKS, PART_BLK), jnp.float32) ** shard_levels(arg_keys[1], (BLOCKS, PART_BLK), ((0, 512),), -0.2, 0.2)), 0.5, 4.0)
    velocity = gaussian(arg_keys[2], (BLOCKS, 3, PART_BLK), 1.0, 6.0, ((0, 512),), jnp.float32)
    block_brick_keys = jax.random.split(jax.random.fold_in(arg_keys[3], 1), BLOCKS // BLK_DEV)
    block_brick_turns = jax.random.permutation(jax.random.fold_in(arg_keys[3], 3), BLOCKS // BLK_DEV)
    block_brick = jax.vmap(lambda own, number: routed_block(jax.random.fold_in(arg_keys[3], 2), own, number, BLK_DEV, N_WIDE, 1, CAP, 2))(block_brick_keys, block_brick_turns).reshape((BLOCKS, 1))
    block_tile = touch_ends(jax.random.randint(arg_keys[4], (BLOCKS,), 0, TILES_DEV), jax.random.fold_in(arg_keys[4], 1), 0, TILES_DEV - 1).astype(jnp.int32)
    fluid_velocity = gaussian(arg_keys[5], (3, NX, NZ, NY), 1.0, 6.0, ((1, 64), (2, 8)), jnp.float32)
    return {"kernel": kernel, "volume": volume, "velocity": velocity, "block_brick": block_brick, "block_tile": block_tile, "fluid_velocity": fluid_velocity}


highest = lax.Precision.HIGHEST


def neighbours(padded):
    return [padded[..., 2:, 1:-1, 1:-1], padded[..., :-2, 1:-1, 1:-1],
            padded[..., 1:-1, 2:, 1:-1], padded[..., 1:-1, :-2, 1:-1],
            padded[..., 1:-1, 1:-1, 2:], padded[..., 1:-1, 1:-1, :-2]]


def to_grid(tiled):
    count = tiled.shape[0]
    shaped = tiled.reshape(count, N_WIDE, N_NARROW, CX, CZ, NY)
    return shaped.transpose(0, 1, 3, 2, 4, 5).reshape(count, NX, NZ, NY)


def from_grid(field):
    count = field.shape[0]
    shaped = field.reshape(count, N_WIDE, CX, N_NARROW, CZ, NY)
    return shaped.transpose(0, 1, 3, 2, 4, 5).reshape(count, N_WIDE * N_NARROW * TILES_DEV, TILE_CELLS)


def pressure_sides(pressure):
    padded = jnp.pad(pressure, 1)
    return neighbours(padded)


def reference(kernel, volume, velocity, block_brick, block_tile, fluid_velocity):
    blocks = kernel.shape[0]
    device = jnp.arange(blocks, dtype=jnp.int32) // BLK_DEV
    slab = device % N_NARROW
    target = (block_brick[:, 0] * N_NARROW + slab) * TILES_DEV + block_tile
    carried = jnp.concatenate([volume[:, None, :], volume[:, None, :] * velocity], axis=1)
    partial_value = jnp.einsum("bkp,bpc->bkc", carried, kernel, precision=highest)
    tile_total = N_WIDE * N_NARROW * TILES_DEV
    summed = jax.ops.segment_sum(partial_value, target, num_segments=tile_total)
    spread = to_grid(summed.transpose(1, 0, 2))
    solid_share = spread[0]
    momentum = spread[1:]
    growth = (1.0 + solid_share) ** 2
    provisional = (fluid_velocity + growth * momentum) / (1.0 + growth * solid_share)
    void_share = 1.0 / (1.0 + solid_share)
    stacked = jnp.concatenate([void_share * provisional, void_share[None]], axis=0)
    sides = neighbours(jnp.pad(stacked, ((0, 0), (1, 1), (1, 1), (1, 1))))
    source = -0.5 * (sides[0][0] - sides[1][0] + sides[2][1] - sides[3][1] + sides[4][2] - sides[5][2])
    weights = [0.5 * (void_share + side[3]) for side in sides]
    diagonal = weights[0] + weights[1] + weights[2] + weights[3] + weights[4] + weights[5]
    pressure = source / diagonal
    for sweep_index in range(SWEEPS - 1):
        beside_all = pressure_sides(pressure)
        total = source
        for which in range(6):
            total = total + weights[which] * beside_all[which]
        pressure = total / diagonal
    beside_all = pressure_sides(pressure)
    fluid_next = provisional - 0.5 * jnp.stack([beside_all[0] - beside_all[1], beside_all[2] - beside_all[3], beside_all[4] - beside_all[5]])
    returned = jnp.concatenate([growth * fluid_next, growth[None]], axis=0)
    picked = from_grid(returned)[:, target]
    sampled = jnp.einsum("kbc,bpc->bkp", picked, kernel, precision=highest)
    particle_drag = volume[:, None, :] * sampled[:, :3] - carried[:, 1:] * sampled[:, 3:4]
    return particle_drag, pressure, fluid_next
```

```python
import functools

import jax
import jax.numpy as jnp
from jax import lax
from jax.experimental import pallas as pl
from jax.experimental.pallas import tpu as pltpu
from jax.sharding import PartitionSpec as P

SWEEPS = 6
DEPTH = SWEEPS + 1
CX, CZ, NY = 4, 8, 512
XS = 2 * CX
XE = XS + 2 * DEPTH
CELLS = 128
SLOTS = 4
KEYS = 4 * SLOTS + 1

highest = lax.Precision.HIGHEST
f32 = jnp.float32


def iota(shape, dim):
    return lax.broadcasted_iota(jnp.int32, shape, dim)


def split3(x):
    hi = x.astype(jnp.bfloat16)
    rest = x - hi.astype(f32)
    mid = rest.astype(jnp.bfloat16)
    low = (rest - mid.astype(f32)).astype(jnp.bfloat16)
    return hi, mid, low


def prev_y(x):
    return jnp.where(iota(x.shape, x.ndim - 1) == 0, 0.0, pltpu.roll(x, 1, x.ndim - 1))


def next_y(x):
    return jnp.where(iota(x.shape, x.ndim - 1) == NY - 1, 0.0, pltpu.roll(x, NY - 1, x.ndim - 1))


def pack_kernel(brick_ref, tile_ref, sums_ref, send_ref, placed_ref, count_ref):
    blocks = sums_ref.shape[0]
    send_ref[...] = jnp.zeros_like(send_ref)

    def clear(i, _):
        count_ref[i] = 0
        return 0

    lax.fori_loop(0, count_ref.shape[0], clear, 0)
    lane = iota((1, CELLS), 1)

    def body(b, _):
        brick = brick_ref[b]
        position = count_ref[brick]
        count_ref[brick] = position + 1
        chip = brick // 2
        slot = (brick % 2) * 2 + position
        placed_ref[b] = chip * SLOTS + slot
        row = chip * KEYS + slot * 4
        for k in range(4):
            send_ref[pl.ds(row + k, 1), :] = sums_ref[b, pl.ds(k, 1), :]
        keys = pl.ds(chip * KEYS + 4 * SLOTS, 1)
        send_ref[keys, :] = jnp.where(lane == slot, tile_ref[b].astype(f32), send_ref[keys, :])
        return 0

    lax.fori_loop(0, blocks, body, 0)


def spread_kernel(recv_ref, fluid_ref, out_ref, pick_ref):
    chips = recv_ref.shape[0] // KEYS
    tiles = recv_ref[pl.ds(4 * SLOTS, chips, stride=KEYS), :].astype(jnp.int32)
    rows = (tiles >> 5) * 32 + (tiles & 3) * 8 + ((tiles >> 2) & 7)
    cells = iota((chips, XS * 32), 1)
    for j in range(SLOTS):
        mine = rows[:, j : j + 1] + (j // 2) * 128
        pick_ref[pl.ds(j * chips, chips), :] = (cells == mine).astype(f32)
    pick = pick_ref[...].astype(jnp.bfloat16)
    for k in range(4):
        sums = jnp.concatenate(
            [recv_ref[pl.ds(j * 4 + k, chips, stride=KEYS), :] for j in range(SLOTS)], axis=0
        )
        total = jnp.zeros((XS * 32, CELLS), f32)
        for part in split3(sums):
            total += lax.dot_general(
                pick, part, (((0,), (0,)), ((), ())), preferred_element_type=f32
            )
        for x in range(XS):
            for q in range(4):
                out_ref[k * XS + x, :, q * 128 : (q + 1) * 128] = total[
                    x * 32 + q * 8 : x * 32 + q * 8 + 8, :
                ]
    out_ref[4 * XS :] = fluid_ref[...].reshape(3 * CX, CZ, NY)


def fields_kernel(core_ref, own_ref, other_ref, field_ref, aux_ref, send_ref):
    core = core_ref[0]
    for x in range(XS):
        sums = [own_ref[k * XS + x] + other_ref[k * XS + x] for k in range(4)]
        mine = core == x // CX
        fluid = [
            jnp.where(
                mine, own_ref[4 * XS + a * CX + x % CX], other_ref[4 * XS + a * CX + x % CX]
            )
            for a in range(3)
        ]
        solid = sums[0]
        growth = (1.0 + solid) ** 2
        void = 1.0 / (1.0 + solid)
        scale = 1.0 / (1.0 + growth * solid)
        provisional = [(fluid[a] + growth * sums[1 + a]) * scale for a in range(3)]
        field_ref[x] = void
        for a in range(3):
            field_ref[(1 + a) * XS + x] = void * provisional[a]
            aux_ref[a * XS + x] = provisional[a]
        aux_ref[3 * XS + x] = growth
    for f in range(4):
        send_ref[f * DEPTH : (f + 1) * DEPTH] = field_ref[pl.ds(f * XS + 1 - core, DEPTH)]


ROWS_S = XE - 2


def source_kernel(core_ref, field_ref, recv_ref, swap_ref, send_ref, face_ref):
    core = core_ref[0]
    first = core == 0

    def row(f, r):
        if r < DEPTH:
            return jnp.where(first, recv_ref[f * DEPTH + r], swap_ref[f * DEPTH + r])
        if r < DEPTH + XS:
            return field_ref[f * XS + r - DEPTH]
        i = f * DEPTH + r - DEPTH - XS
        return jnp.where(first, swap_ref[i], recv_ref[i])

    for r in range(XE):
        send_ref[r] = row(0, r)
    face_ref[...] = jnp.zeros_like(face_ref)
    send_ref[XE + ROWS_S :] = jnp.zeros((3, CZ, NY), f32)
    z = iota((CZ, NY), 0)
    for i in range(ROWS_S):
        r = i + 1
        along_x = row(1, r + 1) - row(1, r - 1)
        vz = row(2, r)
        along_z = jnp.where(z == CZ - 1, 0.0, pltpu.roll(vz, CZ - 1, 0)) - jnp.where(
            z == 0, 0.0, pltpu.roll(vz, 1, 0)
        )
        vy = row(3, r)
        along_y = next_y(vy) - prev_y(vy)
        send_ref[XE + i] = -0.5 * (along_x + along_z + along_y)
        low, high = vz[0:1], vz[CZ - 1 : CZ]
        face_ref[i // 8, i % 8 : i % 8 + 1, :] = low
        face_ref[3 + i // 8, i % 8 : i % 8 + 1, :] = high
        send_ref[XE + ROWS_S + i // 8, i % 8 : i % 8 + 1, :] = jnp.where(first, high, low)


def solve_kernel(
    core_ref, own_ref, face_ref, recv_ref, swap_ref, aux_ref, pick_ref,
    pressure_ref, next_ref, send_ref,
    v, s, wx, wy, wz, inv, pa, pb, coupled,
):
    core = core_ref[0]
    first = core == 0
    mid = pl.ds(CZ, CZ)

    def assemble(r, _):
        here, there = recv_ref[r], swap_ref[r]
        v[r, 0:CZ] = jnp.where(first, here, there)
        v[r, CZ : 2 * CZ] = own_ref[r]
        v[r, 2 * CZ :] = jnp.where(first, there, here)
        return 0

    lax.fori_loop(0, XE, assemble, 0)

    for i in range(ROWS_S):
        r = i + 1
        here, there = recv_ref[XE + i], swap_ref[XE + i]
        s[r, 0:CZ] = jnp.where(first, here, there)
        s[r, CZ : 2 * CZ] = own_ref[XE + i]
        s[r, 2 * CZ :] = jnp.where(first, there, here)
        tile, sub = i // 8, i % 8
        line = slice(sub, sub + 1)
        one = recv_ref[XE + ROWS_S + tile, line, :]
        two = swap_ref[XE + ROWS_S + tile, line, :]
        below, above = jnp.where(first, one, two), jnp.where(first, two, one)
        own_low, own_high = face_ref[tile, line, :], face_ref[3 + tile, line, :]
        s[r, CZ - 1 : CZ] += -0.5 * own_low
        s[r, CZ : CZ + 1] += 0.5 * below
        s[r, 2 * CZ - 1 : 2 * CZ] += -0.5 * above
        s[r, 2 * CZ : 2 * CZ + 1] += 0.5 * own_high

    last = iota((3 * CZ, NY), 1) == NY - 1

    def weights(r, _):
        c = v[r]
        up = next_y(c)
        over = pltpu.roll(c, 3 * CZ - 1, 0)
        diagonal = 3.0 * c + 0.5 * (
            (v[r + 1] + v[r - 1]) + (up + prev_y(c)) + (over + pltpu.roll(c, 1, 0))
        )
        i = jnp.where(c > 0.0, 1.0 / jnp.where(c > 0.0, diagonal, 1.0), 0.0)
        wx[r] = 0.5 * (c + v[r + 1])
        wy[r] = jnp.where(last, 0.0, 0.5 * (c + up))
        wz[r] = 0.5 * (c + over)
        inv[r] = i
        p = s[r] * i
        s[r] = p
        pa[r] = p
        return 0

    lax.fori_loop(1, XE - 1, weights, 0)

    def sweep(src, dst, reach):
        def body(r, _):
            p = src[r]
            y = wy[r]
            z = wz[r]
            acc = wx[r] * src[r + 1] + wx[r - 1] * src[r - 1]
            acc += y * pltpu.roll(p, NY - 1, 1) + pltpu.roll(y * p, 1, 1)
            acc += z * pltpu.roll(p, 3 * CZ - 1, 0) + pltpu.roll(z * p, 1, 0)
            dst[r] = s[r] + inv[r] * acc
            return 0

        lax.fori_loop(DEPTH - reach, DEPTH + XS + reach, body, 0)

    src, dst = pa, pb
    for k in range(1, SWEEPS):
        sweep(src, dst, SWEEPS - k)
        src, dst = dst, src

    for i in range(CX):
        pressure_ref[i] = src[DEPTH + core * CX + i, mid, :]

    for x in range(XS):
        r = DEPTH + x
        p = src[r]
        growth = aux_ref[3 * XS + x]
        diffs = [
            src[r + 1, mid, :] - src[r - 1, mid, :],
            (pltpu.roll(p, 3 * CZ - 1, 0) - pltpu.roll(p, 1, 0))[CZ : 2 * CZ],
            next_y(p[CZ : 2 * CZ]) - prev_y(p[CZ : 2 * CZ]),
        ]
        for a in range(3):
            value = aux_ref[a * XS + x] - 0.5 * diffs[a]
            out = growth * value

            @pl.when(core == x // CX)
            def _(a=a, x=x, value=value):
                next_ref[a, x % CX] = value

            for q in range(4):
                coupled[pl.ds(x * 32 + q * 8, 8), a * 128 : (a + 1) * 128] = out[
                    :, q * 128 : (q + 1) * 128
                ]
        for q in range(4):
            coupled[pl.ds(x * 32 + q * 8, 8), 3 * 128 : 4 * 128] = growth[
                :, q * 128 : (q + 1) * 128
            ]

    pick = pick_ref[...].astype(jnp.bfloat16)
    chips = pick.shape[0] // SLOTS
    for k in range(4):
        total = jnp.zeros((pick.shape[0], CELLS), f32)
        for part in split3(coupled[:, k * 128 : (k + 1) * 128]):
            total += jnp.dot(pick, part, preferred_element_type=f32)
        for j in range(SLOTS):
            send_ref[pl.ds(j * 4 + k, chips, stride=4 * SLOTS), :] = total[
                j * chips : (j + 1) * chips, :
            ]


def gather_kernel(placed_ref, back_ref, out_ref):
    def body(b, _):
        row = placed_ref[b] * 4
        for k in range(4):
            out_ref[b, pl.ds(k, 1), :] = back_ref[pl.ds(row + k, 1), :]
        return 0

    lax.fori_loop(0, out_ref.shape[0], body, 0)


VMEM = pl.BlockSpec(memory_space=pltpu.VMEM)
SMEM = pl.BlockSpec(memory_space=pltpu.SMEM)


def call(kernel, ins, outs, *args, scratch=(), name=None):
    return pl.pallas_call(
        kernel,
        out_shape=[shape for shape, _ in outs],
        in_specs=ins,
        out_specs=[spec for _, spec in outs],
        scratch_shapes=scratch,
        name=name,
        compiler_params=pltpu.CompilerParams(vmem_limit_bytes=40 * 1024 * 1024),
    )(*args)


def arr(*shape):
    return jax.ShapeDtypeStruct(shape, f32)


def local(n_wide, n_narrow, kernel, volume, velocity, block_brick, block_tile, fluid_velocity):
    blocks = kernel.shape[0]
    chips = n_wide // 2
    swap = [(w, w ^ 1) for w in range(n_wide)]
    along_wide = [(w, w + 2) for w in range(0, n_wide - 2, 2)] + [
        (w, w - 2) for w in range(3, n_wide, 2)
    ]
    along_narrow = [
        (w * n_narrow + n, w * n_narrow + t)
        for w in range(n_wide)
        for n in range(n_narrow)
        for t in (n + 1 - 2 * (w % 2),)
        if 0 <= t < n_narrow
    ]
    groups = [list(range(c, n_wide, 2)) for c in range(2)]

    def exchange(x):
        return lax.all_to_all(
            x, "wide", split_axis=0, concat_axis=0, tiled=True, axis_index_groups=groups
        )

    core = (lax.axis_index("wide") % 2).astype(jnp.int32).reshape(1)
    carried = jnp.concatenate([volume[:, None, :], volume[:, None, :] * velocity], axis=1)
    own_sums = jnp.einsum("bkp,bpc->bkc", carried, kernel, precision=highest)
    send, placed = call(
        pack_kernel,
        [SMEM, SMEM, VMEM],
        [(arr(chips * KEYS, CELLS), VMEM), (jax.ShapeDtypeStruct((blocks,), jnp.int32), SMEM)],
        block_brick.reshape(blocks),
        block_tile,
        own_sums,
        scratch=[pltpu.SMEM((n_wide,), jnp.int32)],
        name="pack",
    )
    recv = exchange(send.reshape(chips * KEYS, 1, CELLS)).reshape(chips * KEYS, CELLS)
    part, pick = call(
        spread_kernel,
        [VMEM, VMEM],
        [(arr(4 * XS + 3 * CX, CZ, NY), VMEM), (arr(SLOTS * chips, XS * 32), VMEM)],
        recv,
        fluid_velocity,
        name="spread",
    )
    other = lax.ppermute(part, "wide", swap)
    fields, aux, send_x = call(
        fields_kernel,
        [SMEM, VMEM, VMEM],
        [
            (arr(4 * XS, CZ, NY), VMEM),
            (arr(4 * XS, CZ, NY), VMEM),
            (arr(4 * DEPTH, CZ, NY), VMEM),
        ],
        core,
        part,
        other,
        name="fields",
    )
    recv_x = lax.ppermute(send_x, "wide", along_wide)
    swap_x = lax.ppermute(recv_x, "wide", swap)
    rows_z = XE + ROWS_S + 3
    send_z, faces = call(
        source_kernel,
        [SMEM, VMEM, VMEM, VMEM],
        [(arr(rows_z, CZ, NY), VMEM), (arr(6, CZ, NY), VMEM)],
        core,
        fields,
        recv_x,
        swap_x,
        name="source",
    )
    recv_z = lax.ppermute(send_z, ("wide", "narrow"), along_narrow)
    swap_z = lax.ppermute(recv_z, "wide", swap)
    region = pltpu.VMEM((XE, 3 * CZ, NY), f32)
    pressure, fluid_next, send_back = call(
        solve_kernel,
        [SMEM] + [VMEM] * 6,
        [
            (arr(CX, CZ, NY), VMEM),
            (arr(3, CX, CZ, NY), VMEM),
            (arr(chips * 4 * SLOTS, CELLS), VMEM),
        ],
        core,
        send_z,
        faces,
        recv_z,
        swap_z,
        aux,
        pick,
        scratch=[region] * 8 + [pltpu.VMEM((XS * 32, 4 * CELLS), f32)],
        name="solve",
    )
    back = exchange(send_back.reshape(chips, 4 * SLOTS, CELLS)).reshape(chips * 4 * SLOTS, CELLS)
    (block_fields,) = call(
        gather_kernel,
        [SMEM, VMEM],
        [(arr(blocks, 4, CELLS), VMEM)],
        placed,
        back,
        name="gather",
    )
    sampled = jnp.einsum("bkc,bpc->bkp", block_fields, kernel, precision=highest)
    particle_drag = volume[:, None, :] * sampled[:, :3] - carried[:, 1:] * sampled[:, 3:4]
    return (particle_drag, pressure, fluid_next)


def solution(mesh):
    return jax.shard_map(
        functools.partial(local, mesh.shape["wide"], mesh.shape["narrow"]),
        mesh=mesh,
        in_specs=(
            P(("wide", "narrow"), None, None),
            P(("wide", "narrow"), None),
            P(("wide", "narrow"), None, None),
            P(("wide", "narrow"), None),
            P(("wide", "narrow")),
            P(None, "wide", "narrow", None),
        ),
        out_specs=(
            P(("wide", "narrow"), None, None),
            P("wide", "narrow", None),
            P(None, "wide", "narrow", None),
        ),
        check_vma=False,
    )
```

```python
import functools

import jax
import jax.numpy as jnp
from jax import lax
from jax.experimental import pallas as pl
from jax.experimental.pallas import tpu as pltpu
from jax.sharding import PartitionSpec as P

SWEEPS = 6
DEPTH = SWEEPS + 1
CX, CZ, NY = 4, 8, 512
XS = 2 * CX
XE = XS + 2 * DEPTH
CELLS = 128
SLOTS = 4
KEYS = 4 * SLOTS + 1

high = lax.Precision.HIGH
f32 = jnp.float32
UNROLL = 8


def iota(shape, dim):
    return lax.broadcasted_iota(jnp.int32, shape, dim)


def split3(x):
    hi = x.astype(jnp.bfloat16)
    rest = x - hi.astype(f32)
    mid = rest.astype(jnp.bfloat16)
    low = (rest - mid.astype(f32)).astype(jnp.bfloat16)
    return hi, mid, low


def prev_y(x):
    return jnp.where(iota(x.shape, x.ndim - 1) == 0, 0.0, pltpu.roll(x, 1, x.ndim - 1))


def next_y(x):
    return jnp.where(iota(x.shape, x.ndim - 1) == NY - 1, 0.0, pltpu.roll(x, NY - 1, x.ndim - 1))


def pack_kernel(brick_ref, tile_ref, sums_ref, send_ref, placed_ref, count_ref):
    blocks = sums_ref.shape[0]
    send_ref[...] = jnp.zeros_like(send_ref)

    def clear(i, _):
        count_ref[i] = 0
        return 0

    lax.fori_loop(0, count_ref.shape[0], clear, 0, unroll=8)
    chips = count_ref.shape[0] // 2
    spot = iota((chips, CELLS), 0) * CELLS + iota((chips, CELLS), 1)

    def body(b, keys):
        brick = brick_ref[b]
        position = count_ref[brick]
        count_ref[brick] = position + 1
        chip = brick // 2
        slot = (brick % 2) * 2 + position
        placed_ref[b] = chip * SLOTS + slot
        send_ref[pl.ds(chip * KEYS + slot * 4, 4), :] = sums_ref[b]
        return jnp.where(spot == chip * CELLS + slot, tile_ref[b].astype(f32), keys)

    keys = lax.fori_loop(0, blocks, body, jnp.zeros((chips, CELLS), f32), unroll=UNROLL)
    send_ref[pl.ds(4 * SLOTS, chips, stride=KEYS), :] = keys


def spread_kernel(recv_ref, fluid_ref, out_ref, pick_ref):
    chips = recv_ref.shape[0] // KEYS
    tiles = recv_ref[pl.ds(4 * SLOTS, chips, stride=KEYS), :].astype(jnp.int32)
    rows = (tiles >> 5) * 32 + (tiles & 3) * 8 + ((tiles >> 2) & 7)
    cells = iota((chips, XS * 32), 1)
    for j in range(SLOTS):
        mine = rows[:, j : j + 1] + (j // 2) * 128
        pick_ref[pl.ds(j * chips, chips), :] = (cells == mine).astype(f32)
    pick = pick_ref[...].astype(jnp.bfloat16)
    for k in range(4):
        sums = jnp.concatenate(
            [recv_ref[pl.ds(j * 4 + k, chips, stride=KEYS), :] for j in range(SLOTS)], axis=0
        )
        total = jnp.zeros((XS * 32, CELLS), f32)
        for part in split3(sums):
            total += lax.dot_general(
                pick, part, (((0,), (0,)), ((), ())), preferred_element_type=f32
            )
        for x in range(XS):
            for q in range(4):
                out_ref[k * XS + x, :, q * 128 : (q + 1) * 128] = total[
                    x * 32 + q * 8 : x * 32 + q * 8 + 8, :
                ]
    out_ref[4 * XS :] = fluid_ref[...].reshape(3 * CX, CZ, NY)


def fields_kernel(core_ref, own_ref, other_ref, field_ref, aux_ref, send_ref):
    core = core_ref[0]
    for x in range(XS):
        sums = [own_ref[k * XS + x] + other_ref[k * XS + x] for k in range(4)]
        mine = core == x // CX
        fluid = [
            jnp.where(
                mine, own_ref[4 * XS + a * CX + x % CX], other_ref[4 * XS + a * CX + x % CX]
            )
            for a in range(3)
        ]
        solid = sums[0]
        growth = (1.0 + solid) ** 2
        void = 1.0 / (1.0 + solid)
        scale = 1.0 / (1.0 + growth * solid)
        provisional = [(fluid[a] + growth * sums[1 + a]) * scale for a in range(3)]
        field_ref[x] = void
        for a in range(3):
            field_ref[(1 + a) * XS + x] = void * provisional[a]
            aux_ref[a * XS + x] = provisional[a]
        aux_ref[3 * XS + x] = growth
    for f in range(4):
        send_ref[f * DEPTH : (f + 1) * DEPTH] = field_ref[pl.ds(f * XS + 1 - core, DEPTH)]


ROWS_S = XE - 2


def source_kernel(core_ref, field_ref, recv_ref, swap_ref, send_ref, face_ref):
    core = core_ref[0]
    first = core == 0

    def row(f, r):
        if r < DEPTH:
            return jnp.where(first, recv_ref[f * DEPTH + r], swap_ref[f * DEPTH + r])
        if r < DEPTH + XS:
            return field_ref[f * XS + r - DEPTH]
        i = f * DEPTH + r - DEPTH - XS
        return jnp.where(first, swap_ref[i], recv_ref[i])

    for r in range(XE):
        send_ref[r] = row(0, r)
    face_ref[...] = jnp.zeros_like(face_ref)
    send_ref[XE + ROWS_S :] = jnp.zeros((3, CZ, NY), f32)
    z = iota((CZ, NY), 0)
    for i in range(ROWS_S):
        r = i + 1
        along_x = row(1, r + 1) - row(1, r - 1)
        vz = row(2, r)
        along_z = jnp.where(z == CZ - 1, 0.0, pltpu.roll(vz, CZ - 1, 0)) - jnp.where(
            z == 0, 0.0, pltpu.roll(vz, 1, 0)
        )
        vy = row(3, r)
        along_y = next_y(vy) - prev_y(vy)
        send_ref[XE + i] = -0.5 * (along_x + along_z + along_y)
        low, high = vz[0:1], vz[CZ - 1 : CZ]
        face_ref[i // 8, i % 8 : i % 8 + 1, :] = low
        face_ref[3 + i // 8, i % 8 : i % 8 + 1, :] = high
        send_ref[XE + ROWS_S + i // 8, i % 8 : i % 8 + 1, :] = jnp.where(first, high, low)


ZE = 3 * CZ
Q = NY // CELLS
PAD = 8


def solve_kernel(
    core_ref, own_ref, face_ref, recv_ref, swap_ref, aux_ref, pick_ref,
    pressure_ref, next_ref, send_ref,
    v, s, xp, xm, zp, zm, yp, ym, pa, pb, faces, coupled, keep,
):
    core = core_ref[0]
    lane = iota((CZ, CELLS), 1)
    sub = iota((CZ, CELLS), 0)

    def at(r, q, z=0):
        return pl.ds((r * Q + q) * ZE + PAD + z, CZ)

    def lanes(q):
        return slice(q * CELLS, (q + 1) * CELLS)

    def bring(low, high):
        def body(r, _):
            for q in range(Q):
                v[at(r, q)] = low[r, :, lanes(q)]
                v[at(r, q, CZ)] = own_ref[r, :, lanes(q)]
                v[at(r, q, 2 * CZ)] = high[r, :, lanes(q)]
                s[at(r, q)] = low[XE + r, :, lanes(q)]
                s[at(r, q, CZ)] = own_ref[XE + r, :, lanes(q)]
                s[at(r, q, 2 * CZ)] = high[XE + r, :, lanes(q)]
            return 0

        lax.fori_loop(0, ROWS_S, body, 0, unroll=2)
        for r in range(ROWS_S, XE):
            for q in range(Q):
                v[at(r, q)] = low[r, :, lanes(q)]
                v[at(r, q, CZ)] = own_ref[r, :, lanes(q)]
                v[at(r, q, 2 * CZ)] = high[r, :, lanes(q)]
        tail = XE + ROWS_S
        for f, (ref, base) in enumerate(((face_ref, 0), (face_ref, 3), (low, tail), (high, tail))):
            for t in range(3):
                for q in range(Q):
                    faces[(f * Q + q) * 24 + t * 8 : (f * Q + q) * 24 + t * 8 + 8] = ref[
                        base + t, :, lanes(q)
                    ]

    @pl.when(core == 0)
    def _():
        bring(recv_ref, swap_ref)

    @pl.when(core != 0)
    def _():
        bring(swap_ref, recv_ref)

    def shifted(values):
        up = [pltpu.roll(x, CELLS - 1, 1) for x in values]
        down = [pltpu.roll(x, 1, 1) for x in values]
        ups = [jnp.where(lane == CELLS - 1, up[q + 1], up[q]) for q in range(Q - 1)] + [up[-1]]
        downs = [down[0]] + [jnp.where(lane == 0, down[q - 1], down[q]) for q in range(1, Q)]
        return ups, downs

    def weights(r, _):
        i = r - 1

        def face(f, q):
            return jnp.broadcast_to(faces[pl.ds((f * Q + q) * 24 + i, 1)], (CZ, CELLS))

        for z in range(0, ZE, CZ):
            c = [v[at(r, q, z)] for q in range(Q)]
            ups, downs = shifted(c)
            for q in range(Q):
                up, down = ups[q], downs[q]
                if q == Q - 1:
                    up = jnp.where(lane == CELLS - 1, 0.0, up)
                if q == 0:
                    down = jnp.where(lane == 0, 0.0, down)
                here = at(r, q, z)
                t = [
                    c[q] + v[at(r + 1, q, z)],
                    c[q] + v[at(r - 1, q, z)],
                    c[q] + v[at(r, q, z + 1)],
                    c[q] + v[at(r, q, z - 1)],
                    c[q] + up,
                    c[q] + down,
                ]
                total = ((t[0] + t[1]) + (t[2] + t[3])) + (t[4] + t[5])
                some = c[q] > 0.0
                scale = jnp.where(some, 1.0 / jnp.where(some, total, 1.0), 0.0)
                if q == Q - 1:
                    t[4] = jnp.where(lane == CELLS - 1, 0.0, t[4])
                if q == 0:
                    t[5] = jnp.where(lane == 0, 0.0, t[5])
                for ref, value in zip((xp, xm, zp, zm, yp, ym), t):
                    ref[here] = value * scale
                value = s[at(i, q, z)]
                if z == 0:
                    value = value - jnp.where(sub == CZ - 1, 0.5 * face(0, q), 0.0)
                elif z == CZ:
                    value = value + jnp.where(sub == 0, 0.5 * face(2, q), 0.0)
                    value = value - jnp.where(sub == CZ - 1, 0.5 * face(3, q), 0.0)
                else:
                    value = value + jnp.where(sub == 0, 0.5 * face(1, q), 0.0)
                value = (2.0 * value) * scale
                s[at(i, q, z)] = value
                pa[here] = value
        return 0

    lax.fori_loop(1, XE - 1, weights, 0)

    def sweep(src, dst, reach):
        def body(r, _):
            for z in range(0, ZE, CZ):
                p = [src[at(r, q, z)] for q in range(Q)]
                ups, downs = shifted(p)
                for q in range(Q):
                    here = at(r, q, z)
                    a = xp[here] * src[at(r + 1, q, z)] + xm[here] * src[at(r - 1, q, z)]
                    b = zp[here] * src[at(r, q, z + 1)] + zm[here] * src[at(r, q, z - 1)]
                    c = yp[here] * ups[q] + ym[here] * downs[q]
                    dst[here] = (s[at(r - 1, q, z)] + a) + (b + c)
            return 0

        lax.fori_loop(DEPTH - reach, DEPTH + XS + reach, body, 0, unroll=2)

    src, dst = pa, pb
    for k in range(1, SWEEPS):
        sweep(src, dst, SWEEPS - k)
        src, dst = dst, src

    for i in range(CX):
        for q in range(Q):
            pressure_ref[i, :, lanes(q)] = src[at(DEPTH + core * CX + i, q, CZ)]
    for x in range(XS):
        r = DEPTH + x
        p = [src[at(r, q, CZ)] for q in range(Q)]
        ups, downs = shifted(p)
        ups[-1] = jnp.where(lane == CELLS - 1, 0.0, ups[-1])
        downs[0] = jnp.where(lane == 0, 0.0, downs[0])
        for q in range(Q):
            growth = aux_ref[3 * XS + x, :, lanes(q)]
            diffs = [
                src[at(r + 1, q, CZ)] - src[at(r - 1, q, CZ)],
                src[at(r, q, CZ + 1)] - src[at(r, q, CZ - 1)],
                ups[q] - downs[q],
            ]
            put = slice(x * 32 + q * 8, x * 32 + q * 8 + 8)
            for a in range(3):
                value = aux_ref[a * XS + x, :, lanes(q)] - 0.5 * diffs[a]
                coupled[put, lanes(a)] = growth * value
                keep[a * XS + x, :, lanes(q)] = value
            coupled[put, lanes(3)] = growth
    for a in range(3):
        next_ref[a] = keep[pl.ds(a * XS + core * CX, CX)]

    pick = pick_ref[...].astype(jnp.bfloat16)
    chips = pick.shape[0] // SLOTS
    for k in range(4):
        total = jnp.zeros((pick.shape[0], CELLS), f32)
        for part in split3(coupled[:, lanes(k)]):
            total += jnp.dot(pick, part, preferred_element_type=f32)
        for j in range(SLOTS):
            send_ref[pl.ds(j * 4 + k, chips, stride=4 * SLOTS), :] = total[
                j * chips : (j + 1) * chips, :
            ]


def gather_kernel(placed_ref, back_ref, out_ref):
    def body(b, _):
        out_ref[b] = back_ref[pl.ds(placed_ref[b] * 4, 4), :]
        return 0

    lax.fori_loop(0, out_ref.shape[0], body, 0, unroll=UNROLL)


VMEM = pl.BlockSpec(memory_space=pltpu.VMEM)
SMEM = pl.BlockSpec(memory_space=pltpu.SMEM)


def call(kernel, ins, outs, *args, scratch=(), name=None, grant=4):
    return pl.pallas_call(
        kernel,
        out_shape=[shape for shape, _ in outs],
        in_specs=ins,
        out_specs=[spec for _, spec in outs],
        scratch_shapes=scratch,
        name=name,
        compiler_params=pltpu.CompilerParams(vmem_limit_bytes=grant * 1024 * 1024),
    )(*args)


def arr(*shape):
    return jax.ShapeDtypeStruct(shape, f32)


def local(n_wide, n_narrow, kernel, volume, velocity, block_brick, block_tile, fluid_velocity):
    blocks = kernel.shape[0]
    chips = n_wide // 2
    swap = [(w, w ^ 1) for w in range(n_wide)]
    along_wide = [(w, w + 2) for w in range(0, n_wide - 2, 2)] + [
        (w, w - 2) for w in range(3, n_wide, 2)
    ]
    along_narrow = [
        (w * n_narrow + n, w * n_narrow + t)
        for w in range(n_wide)
        for n in range(n_narrow)
        for t in (n + 1 - 2 * (w % 2),)
        if 0 <= t < n_narrow
    ]
    groups = [list(range(c, n_wide, 2)) for c in range(2)]

    def exchange(x):
        return lax.all_to_all(
            x, "wide", split_axis=0, concat_axis=0, tiled=True, axis_index_groups=groups
        )

    core = (lax.axis_index("wide") % 2).astype(jnp.int32).reshape(1)
    carried = jnp.concatenate([volume[:, None, :], volume[:, None, :] * velocity], axis=1)
    own_sums = jnp.einsum("bkp,bpc->bkc", carried, kernel, precision=high)
    send, placed = call(
        pack_kernel,
        [SMEM, SMEM, VMEM],
        [(arr(chips * KEYS, CELLS), VMEM), (jax.ShapeDtypeStruct((blocks,), jnp.int32), SMEM)],
        block_brick.reshape(blocks),
        block_tile,
        own_sums,
        scratch=[pltpu.SMEM((n_wide,), jnp.int32)],
        name="pack",
    )
    recv = exchange(send.reshape(chips * KEYS, 1, CELLS)).reshape(chips * KEYS, CELLS)
    part, pick = call(
        spread_kernel,
        [VMEM, VMEM],
        [(arr(4 * XS + 3 * CX, CZ, NY), VMEM), (arr(SLOTS * chips, XS * 32), VMEM)],
        recv,
        fluid_velocity,
        name="spread",
    )
    other = lax.ppermute(part, "wide", swap)
    fields, aux, send_x = call(
        fields_kernel,
        [SMEM, VMEM, VMEM],
        [
            (arr(4 * XS, CZ, NY), VMEM),
            (arr(4 * XS, CZ, NY), VMEM),
            (arr(4 * DEPTH, CZ, NY), VMEM),
        ],
        core,
        part,
        other,
        name="fields",
    )
    recv_x = lax.ppermute(send_x, "wide", along_wide)
    swap_x = lax.ppermute(recv_x, "wide", swap)
    rows_z = XE + ROWS_S + 3
    send_z, faces = call(
        source_kernel,
        [SMEM, VMEM, VMEM, VMEM],
        [(arr(rows_z, CZ, NY), VMEM), (arr(6, CZ, NY), VMEM)],
        core,
        fields,
        recv_x,
        swap_x,
        name="source",
    )
    recv_z = lax.ppermute(send_z, ("wide", "narrow"), along_narrow)
    swap_z = lax.ppermute(recv_z, "wide", swap)
    region = pltpu.VMEM((XE * Q * ZE + 2 * PAD, CELLS), f32)
    pressure, fluid_next, send_back = call(
        solve_kernel,
        [SMEM] + [VMEM] * 6,
        [
            (arr(CX, CZ, NY), VMEM),
            (arr(3, CX, CZ, NY), VMEM),
            (arr(chips * 4 * SLOTS, CELLS), VMEM),
        ],
        core,
        send_z,
        faces,
        recv_z,
        swap_z,
        aux,
        pick,
        scratch=[region] * 10
        + [
            pltpu.VMEM((4 * Q * 24 + PAD, CELLS), f32),
            pltpu.VMEM((XS * 32, 4 * CELLS), f32),
            pltpu.VMEM((3 * XS, CZ, NY), f32),
        ],
        name="solve",
        grant=20,
    )
    back = exchange(send_back.reshape(chips, 4 * SLOTS, CELLS)).reshape(chips * 4 * SLOTS, CELLS)
    (block_fields,) = call(
        gather_kernel,
        [SMEM, VMEM],
        [(arr(blocks, 4, CELLS), VMEM)],
        placed,
        back,
        name="gather",
    )
    sampled = jnp.einsum("bkc,bpc->bkp", block_fields, kernel, precision=high)
    particle_drag = volume[:, None, :] * sampled[:, :3] - carried[:, 1:] * sampled[:, 3:4]
    return (particle_drag, pressure, fluid_next)


def solution(mesh):
    return jax.shard_map(
        functools.partial(local, mesh.shape["wide"], mesh.shape["narrow"]),
        mesh=mesh,
        in_specs=(
            P(("wide", "narrow"), None, None),
            P(("wide", "narrow"), None),
            P(("wide", "narrow"), None, None),
            P(("wide", "narrow"), None),
            P(("wide", "narrow")),
            P(None, "wide", "narrow", None),
        ),
        out_specs=(
            P(("wide", "narrow"), None, None),
            P("wide", "narrow", None),
            P(None, "wide", "narrow", None),
        ),
        check_vma=False,
    )
```

```python
import functools

import jax
import jax.numpy as jnp
from jax import lax
from jax.experimental import pallas as pl
from jax.experimental.pallas import tpu as pltpu
from jax.sharding import PartitionSpec as P

SWEEPS = 6
DEPTH = SWEEPS + 1
CX, CZ, NY = 4, 8, 512
XS = 2 * CX
XE = XS + 2 * DEPTH
CELLS = 128
SLOTS = 4
KEYS = 4 * SLOTS + 1

high = lax.Precision.HIGH
f32 = jnp.float32
UNROLL = 8


def iota(shape, dim):
    return lax.broadcasted_iota(jnp.int32, shape, dim)


def split3(x):
    hi = x.astype(jnp.bfloat16)
    rest = x - hi.astype(f32)
    mid = rest.astype(jnp.bfloat16)
    low = (rest - mid.astype(f32)).astype(jnp.bfloat16)
    return hi, mid, low


def prev_y(x):
    return jnp.where(iota(x.shape, x.ndim - 1) == 0, 0.0, pltpu.roll(x, 1, x.ndim - 1))


def next_y(x):
    return jnp.where(iota(x.shape, x.ndim - 1) == NY - 1, 0.0, pltpu.roll(x, NY - 1, x.ndim - 1))


def pack_kernel(brick_ref, tile_ref, sums_ref, send_ref, placed_ref, count_ref):
    blocks = sums_ref.shape[0]
    send_ref[...] = jnp.zeros_like(send_ref)

    def clear(i, _):
        count_ref[i] = 0
        return 0

    lax.fori_loop(0, count_ref.shape[0], clear, 0, unroll=8)
    chips = count_ref.shape[0] // 2
    spot = iota((chips, CELLS), 0) * CELLS + iota((chips, CELLS), 1)

    def body(b, keys):
        brick = brick_ref[b]
        position = count_ref[brick]
        count_ref[brick] = position + 1
        chip = brick // 2
        slot = (brick % 2) * 2 + position
        placed_ref[b] = chip * SLOTS + slot
        send_ref[pl.ds(chip * KEYS + slot * 4, 4), :] = sums_ref[b]
        return jnp.where(spot == chip * CELLS + slot, tile_ref[b].astype(f32), keys)

    keys = lax.fori_loop(0, blocks, body, jnp.zeros((chips, CELLS), f32), unroll=UNROLL)
    send_ref[pl.ds(4 * SLOTS, chips, stride=KEYS), :] = keys


def picking(tiles, pick_ref):
    chips = tiles.shape[0]
    tiles = tiles.astype(jnp.int32)
    rows = (tiles >> 5) * 32 + (tiles & 3) * 8 + ((tiles >> 2) & 7)
    cells = iota((chips, XS * 32), 1)
    for j in range(SLOTS):
        mine = rows[:, j : j + 1] + (j // 2) * 128
        pick_ref[pl.ds(j * chips, chips), :] = (cells == mine).astype(f32)


def spread_kernel(recv_ref, fluid_ref, out_ref, pick_ref):
    chips = recv_ref.shape[0] // KEYS
    tiles = recv_ref[pl.ds(4 * SLOTS, chips, stride=KEYS), :]
    picking(tiles, pick_ref)
    for q in range(chips // CZ):
        out_ref[4 * XS + 3 * CX, :, q * CELLS : (q + 1) * CELLS] = tiles[q * CZ : (q + 1) * CZ]
    pick = pick_ref[...].astype(jnp.bfloat16)
    for k in range(4):
        sums = jnp.concatenate(
            [recv_ref[pl.ds(j * 4 + k, chips, stride=KEYS), :] for j in range(SLOTS)], axis=0
        )
        total = jnp.zeros((XS * 32, CELLS), f32)
        for part in split3(sums):
            total += lax.dot_general(
                pick, part, (((0,), (0,)), ((), ())), preferred_element_type=f32
            )
        for x in range(XS):
            for q in range(4):
                out_ref[k * XS + x, :, q * 128 : (q + 1) * 128] = total[
                    x * 32 + q * 8 : x * 32 + q * 8 + 8, :
                ]
    out_ref[4 * XS : 4 * XS + 3 * CX] = fluid_ref[...].reshape(3 * CX, CZ, NY)


ROWS_S = XE - 2
MSG_X = DEPTH + (DEPTH - 1) + 3
PACK_V = (((1, 0), (5, 6)), ((2, 0), (4, 5)), ((3, 0), (6, 4)))
PACK_S = (((1, 0), (3, 5)), ((2, 0), (4, 4), (5, 6)))
MSG_Z = 2 * XS + 2 * (len(PACK_V) + len(PACK_S)) + 3
FACES_Z = MSG_Z - 3


def place(x, start, to, count):
    line = iota(x.shape, 0)
    shift = (to - start) % CZ
    moved = pltpu.roll(x, shift, 0) if shift else x
    return jnp.where((line >= to) & (line < to + count), moved, 0.0)


def packed_rows():
    tile = 2 * XS
    for plan, reach in ((PACK_V, DEPTH), (PACK_S, DEPTH - 1)):
        for side in range(2):
            for group in plan:
                yield tile, reach, [
                    (DEPTH - d if side == 0 else DEPTH + XS - 1 + d, line, reach - d)
                    for d, line in group
                ]
                tile += 1


def fields_kernel(core_ref, own_ref, other_ref, field_ref, aux_ref, send_ref, vx, vz):
    core = core_ref[0]
    z = iota((CZ, NY), 0)
    aux_ref[4 * XS] = own_ref[4 * XS + 3 * CX]
    for x in range(XS):
        sums = [own_ref[k * XS + x] + other_ref[k * XS + x] for k in range(4)]
        mine = core == x // CX
        fluid = [
            jnp.where(
                mine, own_ref[4 * XS + a * CX + x % CX], other_ref[4 * XS + a * CX + x % CX]
            )
            for a in range(3)
        ]
        solid = sums[0]
        growth = (1.0 + solid) ** 2
        void = 1.0 / (1.0 + solid)
        scale = 1.0 / (1.0 + growth * solid)
        provisional = [(fluid[a] + growth * sums[1 + a]) * scale for a in range(3)]
        field_ref[x] = void
        for a in range(3):
            aux_ref[a * XS + x] = provisional[a]
        aux_ref[3 * XS + x] = growth
        vx[x] = void * provisional[0]
        vz[x] = void * provisional[1]
        along_z = vz[x]
        along_y = void * provisional[2]
        field_ref[XS + x] = -0.5 * (
            jnp.where(z == CZ - 1, 0.0, pltpu.roll(along_z, CZ - 1, 0))
            - jnp.where(z == 0, 0.0, pltpu.roll(along_z, 1, 0))
            + next_y(along_y)
            - prev_y(along_y)
        )
    for x in range(XS):
        if x == 0:
            along_x = vx[1]
        elif x == XS - 1:
            along_x = -vx[XS - 2]
        else:
            along_x = vx[x + 1] - vx[x - 1]
        field_ref[XS + x] = field_ref[XS + x] - 0.5 * along_x
        field_ref[2 * XS + 2, x : x + 1, :] = vz[x, 0:1, :]
        field_ref[2 * XS + 3, x : x + 1, :] = vz[x, CZ - 1 : CZ, :]
    field_ref[2 * XS] = vx[0]
    field_ref[2 * XS + 1] = vx[XS - 1]

    def fill(where):
        for d in range(1, DEPTH + 1):
            send_ref[d - 1] = field_ref[where(d)]
        for d in range(1, DEPTH):
            send_ref[DEPTH + d - 1] = field_ref[XS + where(d)]
        send_ref[2 * DEPTH - 1] = vx[where(1)]
        for f in range(2):
            tile = 2 * DEPTH + f
            send_ref[tile] = jnp.zeros((CZ, NY), f32)
            for d in range(1, DEPTH):
                x = where(d)
                send_ref[tile, d - 1 : d, :] = field_ref[2 * XS + 2 + f, x : x + 1, :]

    @pl.when(core == 0)
    def _():
        fill(lambda d: XS - d)

    @pl.when(core != 0)
    def _():
        fill(lambda d: d - 1)


def source_kernel(core_ref, field_ref, recv_ref, swap_ref, send_ref, face_ref, v, s):
    core = core_ref[0]

    def bring(low, high):
        for d in range(1, DEPTH + 1):
            v[DEPTH - d] = low[d - 1]
            v[DEPTH + XS - 1 + d] = high[d - 1]
        for x in range(XS):
            v[DEPTH + x] = field_ref[x]
            s[DEPTH + x] = field_ref[XS + x]
        for d in range(1, DEPTH):
            s[DEPTH - d] = low[DEPTH + d - 1]
            s[DEPTH + XS - 1 + d] = high[DEPTH + d - 1]
        edge = 2 * DEPTH - 1
        s[DEPTH - 1] = s[DEPTH - 1] - 0.5 * field_ref[2 * XS]
        s[DEPTH] = s[DEPTH] + 0.5 * low[edge]
        s[DEPTH + XS - 1] = s[DEPTH + XS - 1] - 0.5 * high[edge]
        s[DEPTH + XS] = s[DEPTH + XS] + 0.5 * field_ref[2 * XS + 1]
        for f in range(2):
            face_ref[3 * f + 2] = jnp.zeros((CZ, NY), f32)
            for i in range(ROWS_S):
                r = i + 1
                if r < DEPTH:
                    d = DEPTH - r
                    value = low[2 * DEPTH + f, d - 1 : d, :]
                elif r < DEPTH + XS:
                    x = r - DEPTH
                    value = field_ref[2 * XS + 2 + f, x : x + 1, :]
                else:
                    d = r - DEPTH - XS + 1
                    value = high[2 * DEPTH + f, d - 1 : d, :]
                face_ref[3 * f + i // 8, i % 8 : i % 8 + 1, :] = value

    @pl.when(core == 0)
    def _():
        bring(recv_ref, swap_ref)

    @pl.when(core != 0)
    def _():
        bring(swap_ref, recv_ref)

    for x in range(XS):
        send_ref[x] = v[DEPTH + x]
        send_ref[XS + x] = s[DEPTH + x]

    def fill(up):
        for tile, reach, rows in packed_rows():
            ref = v if reach == DEPTH else s
            total = None
            for r, line, count in rows:
                part = place(ref[r], CZ - count if up else 0, line, count)
                total = part if total is None else total + part
            send_ref[tile] = total
        for t in range(3):
            send_ref[FACES_Z + t] = face_ref[(3 if up else 0) + t]

    @pl.when(core == 0)
    def _():
        fill(True)

    @pl.when(core != 0)
    def _():
        fill(False)


ZE = 3 * CZ
Q = NY // CELLS
PAD = 8


def solve_kernel(
    core_ref, v_ref, s_ref, face_ref, recv_ref, swap_ref, aux_ref,
    pressure_ref, next_ref, send_ref,
    v, s, xp, xm, zp, zm, yp, ym, pa, pb, faces, coupled, keep, pick_ref,
):
    core = core_ref[0]
    lane = iota((CZ, CELLS), 1)
    sub = iota((CZ, CELLS), 0)

    def at(r, q, z=0):
        return pl.ds((r * Q + q) * ZE + PAD + z, CZ)

    def lanes(q):
        return slice(q * CELLS, (q + 1) * CELLS)

    def bring(low, high):
        none = jnp.zeros((CZ, CELLS), f32)
        for q in range(Q):
            for r in (0, XE - 1):
                v[at(r, q)] = none
                v[at(r, q, 2 * CZ)] = none
            for r in (1, XE - 2):
                s[at(r - 1, q)] = none
                s[at(r - 1, q, 2 * CZ)] = none
            for r in range(XE):
                v[at(r, q, CZ)] = v_ref[r, :, lanes(q)]
            for i in range(ROWS_S):
                s[at(i, q, CZ)] = s_ref[i + 1, :, lanes(q)]
            for x in range(XS):
                v[at(DEPTH + x, q)] = low[x, :, lanes(q)]
                v[at(DEPTH + x, q, 2 * CZ)] = high[x, :, lanes(q)]
                s[at(DEPTH + x - 1, q)] = low[XS + x, :, lanes(q)]
                s[at(DEPTH + x - 1, q, 2 * CZ)] = high[XS + x, :, lanes(q)]
            for tile, reach, rows in packed_rows():
                a, b = low[tile, :, lanes(q)], high[tile, :, lanes(q)]
                for r, line, count in rows:
                    ref, i = (v, r) if reach == DEPTH else (s, r - 1)
                    ref[at(i, q)] = place(a, line, CZ - count, count)
                    ref[at(i, q, 2 * CZ)] = place(b, line, 0, count)
        for f, (ref, base) in enumerate(
            ((face_ref, 0), (face_ref, 3), (low, FACES_Z), (high, FACES_Z))
        ):
            for t in range(3):
                for q in range(Q):
                    faces[(f * Q + q) * 24 + t * 8 : (f * Q + q) * 24 + t * 8 + 8] = ref[
                        base + t, :, lanes(q)
                    ]

    @pl.when(core == 0)
    def _():
        bring(recv_ref, swap_ref)

    @pl.when(core != 0)
    def _():
        bring(swap_ref, recv_ref)

    def shifted(values):
        up = [pltpu.roll(x, CELLS - 1, 1) for x in values]
        down = [pltpu.roll(x, 1, 1) for x in values]
        ups = [jnp.where(lane == CELLS - 1, up[q + 1], up[q]) for q in range(Q - 1)] + [up[-1]]
        downs = [down[0]] + [jnp.where(lane == 0, down[q - 1], down[q]) for q in range(1, Q)]
        return ups, downs

    def weights(r, _):
        i = r - 1

        def face(f, q):
            return jnp.broadcast_to(faces[pl.ds((f * Q + q) * 24 + i, 1)], (CZ, CELLS))

        for z in range(0, ZE, CZ):
            c = [v[at(r, q, z)] for q in range(Q)]
            ups, downs = shifted(c)
            for q in range(Q):
                up, down = ups[q], downs[q]
                if q == Q - 1:
                    up = jnp.where(lane == CELLS - 1, 0.0, up)
                if q == 0:
                    down = jnp.where(lane == 0, 0.0, down)
                here = at(r, q, z)
                t = [
                    c[q] + v[at(r + 1, q, z)],
                    c[q] + v[at(r - 1, q, z)],
                    c[q] + v[at(r, q, z + 1)],
                    c[q] + v[at(r, q, z - 1)],
                    c[q] + up,
                    c[q] + down,
                ]
                total = ((t[0] + t[1]) + (t[2] + t[3])) + (t[4] + t[5])
                some = c[q] > 0.0
                scale = jnp.where(some, 1.0 / jnp.where(some, total, 1.0), 0.0)
                if q == Q - 1:
                    t[4] = jnp.where(lane == CELLS - 1, 0.0, t[4])
                if q == 0:
                    t[5] = jnp.where(lane == 0, 0.0, t[5])
                for ref, value in zip((xp, xm, zp, zm, yp, ym), t):
                    ref[here] = value * scale
                value = s[at(i, q, z)]
                if z == 0:
                    value = value - jnp.where(sub == CZ - 1, 0.5 * face(0, q), 0.0)
                elif z == CZ:
                    value = value + jnp.where(sub == 0, 0.5 * face(2, q), 0.0)
                    value = value - jnp.where(sub == CZ - 1, 0.5 * face(3, q), 0.0)
                else:
                    value = value + jnp.where(sub == 0, 0.5 * face(1, q), 0.0)
                value = (2.0 * value) * scale
                s[at(i, q, z)] = value
                pa[here] = value
        return 0

    for r in range(1, XE - 1):
        weights(r, 0)

    def sweep(src, dst, reach):
        def body(r, _):
            for z in range(0, ZE, CZ):
                p = [src[at(r, q, z)] for q in range(Q)]
                ups, downs = shifted(p)
                for q in range(Q):
                    here = at(r, q, z)
                    a = xp[here] * src[at(r + 1, q, z)] + xm[here] * src[at(r - 1, q, z)]
                    b = zp[here] * src[at(r, q, z + 1)] + zm[here] * src[at(r, q, z - 1)]
                    c = yp[here] * ups[q] + ym[here] * downs[q]
                    dst[here] = (s[at(r - 1, q, z)] + a) + (b + c)
            return 0

        for r in range(DEPTH - reach, DEPTH + XS + reach):
            body(r, 0)

    src, dst = pa, pb
    for k in range(1, SWEEPS):
        sweep(src, dst, SWEEPS - k)
        src, dst = dst, src

    for i in range(CX):
        for q in range(Q):
            pressure_ref[i, :, lanes(q)] = src[at(DEPTH + core * CX + i, q, CZ)]
    for x in range(XS):
        r = DEPTH + x
        p = [src[at(r, q, CZ)] for q in range(Q)]
        ups, downs = shifted(p)
        ups[-1] = jnp.where(lane == CELLS - 1, 0.0, ups[-1])
        downs[0] = jnp.where(lane == 0, 0.0, downs[0])
        for q in range(Q):
            growth = aux_ref[3 * XS + x, :, lanes(q)]
            diffs = [
                src[at(r + 1, q, CZ)] - src[at(r - 1, q, CZ)],
                src[at(r, q, CZ + 1)] - src[at(r, q, CZ - 1)],
                ups[q] - downs[q],
            ]
            put = slice(x * 32 + q * 8, x * 32 + q * 8 + 8)
            for a in range(3):
                value = aux_ref[a * XS + x, :, lanes(q)] - 0.5 * diffs[a]
                coupled[put, lanes(a)] = growth * value
                keep[a * XS + x, :, lanes(q)] = value
            coupled[put, lanes(3)] = growth
    for a in range(3):
        next_ref[a] = keep[pl.ds(a * XS + core * CX, CX)]

    chips = pick_ref.shape[0] // SLOTS
    tiles = aux_ref[4 * XS]
    picking(jnp.concatenate([tiles[:, lanes(q)] for q in range(chips // CZ)], axis=0), pick_ref)
    pick = pick_ref[...].astype(jnp.bfloat16)
    for k in range(4):
        total = jnp.zeros((pick.shape[0], CELLS), f32)
        for part in split3(coupled[:, lanes(k)]):
            total += jnp.dot(pick, part, preferred_element_type=f32)
        for j in range(SLOTS):
            send_ref[pl.ds(j * 4 + k, chips, stride=4 * SLOTS), :] = total[
                j * chips : (j + 1) * chips, :
            ]


def gather_kernel(placed_ref, back_ref, out_ref):
    def body(b, _):
        out_ref[b] = back_ref[pl.ds(placed_ref[b] * 4, 4), :]
        return 0

    lax.fori_loop(0, out_ref.shape[0], body, 0, unroll=UNROLL)


VMEM = pl.BlockSpec(memory_space=pltpu.VMEM)
SMEM = pl.BlockSpec(memory_space=pltpu.SMEM)


def call(kernel, ins, outs, *args, scratch=(), name=None, grant=4):
    return pl.pallas_call(
        kernel,
        out_shape=[shape for shape, _ in outs],
        in_specs=ins,
        out_specs=[spec for _, spec in outs],
        scratch_shapes=scratch,
        name=name,
        compiler_params=pltpu.CompilerParams(vmem_limit_bytes=grant * 1024 * 1024),
    )(*args)


def arr(*shape):
    return jax.ShapeDtypeStruct(shape, f32)


def local(n_wide, n_narrow, kernel, volume, velocity, block_brick, block_tile, fluid_velocity):
    blocks = kernel.shape[0]
    chips = n_wide // 2
    swap = [(w, w ^ 1) for w in range(n_wide)]
    along_wide = [(w, w + 2) for w in range(0, n_wide - 2, 2)] + [
        (w, w - 2) for w in range(3, n_wide, 2)
    ]
    along_narrow = [
        (w * n_narrow + n, w * n_narrow + t)
        for w in range(n_wide)
        for n in range(n_narrow)
        for t in (n + 1 - 2 * (w % 2),)
        if 0 <= t < n_narrow
    ]
    groups = [list(range(c, n_wide, 2)) for c in range(2)]

    def exchange(x):
        return lax.all_to_all(
            x, "wide", split_axis=0, concat_axis=0, tiled=True, axis_index_groups=groups
        )

    core = (lax.axis_index("wide") % 2).astype(jnp.int32).reshape(1)
    carried = jnp.concatenate([volume[:, None, :], volume[:, None, :] * velocity], axis=1)
    own_sums = jnp.einsum("bkp,bpc->bkc", carried, kernel, precision=high)
    send, placed = call(
        pack_kernel,
        [SMEM, SMEM, VMEM],
        [(arr(chips * KEYS, CELLS), VMEM), (jax.ShapeDtypeStruct((blocks,), jnp.int32), SMEM)],
        block_brick.reshape(blocks),
        block_tile,
        own_sums,
        scratch=[pltpu.SMEM((n_wide,), jnp.int32)],
        name="pack",
    )
    recv = exchange(send.reshape(chips * KEYS, 1, CELLS)).reshape(chips * KEYS, CELLS)
    (part,) = call(
        spread_kernel,
        [VMEM, VMEM],
        [(arr(4 * XS + 3 * CX + 1, CZ, NY), VMEM)],
        recv,
        fluid_velocity,
        scratch=[pltpu.VMEM((SLOTS * chips, XS * 32), f32)],
        name="spread",
    )
    other = lax.ppermute(part, "wide", swap)
    fields, aux, send_x = call(
        fields_kernel,
        [SMEM, VMEM, VMEM],
        [
            (arr(2 * XS + 4, CZ, NY), VMEM),
            (arr(4 * XS + 1, CZ, NY), VMEM),
            (arr(MSG_X, CZ, NY), VMEM),
        ],
        core,
        part,
        other,
        scratch=[pltpu.VMEM((XS, CZ, NY), f32)] * 2,
        name="fields",
    )
    recv_x = lax.ppermute(send_x, "wide", along_wide)
    swap_x = lax.ppermute(recv_x, "wide", swap)
    send_z, faces, void, source = call(
        source_kernel,
        [SMEM, VMEM, VMEM, VMEM],
        [
            (arr(MSG_Z, CZ, NY), VMEM),
            (arr(6, CZ, NY), VMEM),
            (arr(XE, CZ, NY), VMEM),
            (arr(XE - 1, CZ, NY), VMEM),
        ],
        core,
        fields,
        recv_x,
        swap_x,
        name="source",
    )
    recv_z = lax.ppermute(send_z, ("wide", "narrow"), along_narrow)
    swap_z = lax.ppermute(recv_z, "wide", swap)
    region = pltpu.VMEM((XE * Q * ZE + 2 * PAD, CELLS), f32)
    pressure, fluid_next, send_back = call(
        solve_kernel,
        [SMEM] + [VMEM] * 6,
        [
            (arr(CX, CZ, NY), VMEM),
            (arr(3, CX, CZ, NY), VMEM),
            (arr(chips * 4 * SLOTS, CELLS), VMEM),
        ],
        core,
        void,
        source,
        faces,
        recv_z,
        swap_z,
        aux,
        scratch=[region] * 10
        + [
            pltpu.VMEM((4 * Q * 24 + PAD, CELLS), f32),
            pltpu.VMEM((XS * 32, 4 * CELLS), f32),
            pltpu.VMEM((3 * XS, CZ, NY), f32),
            pltpu.VMEM((SLOTS * chips, XS * 32), f32),
        ],
        name="solve",
        grant=20,
    )
    back = exchange(send_back.reshape(chips, 4 * SLOTS, CELLS)).reshape(chips * 4 * SLOTS, CELLS)
    (block_fields,) = call(
        gather_kernel,
        [SMEM, VMEM],
        [(arr(blocks, 4, CELLS), VMEM)],
        placed,
        back,
        name="gather",
    )
    sampled = jnp.einsum("bkc,bpc->bkp", block_fields, kernel, precision=high)
    particle_drag = volume[:, None, :] * sampled[:, :3] - carried[:, 1:] * sampled[:, 3:4]
    return (particle_drag, pressure, fluid_next)


def solution(mesh):
    return jax.shard_map(
        functools.partial(local, mesh.shape["wide"], mesh.shape["narrow"]),
        mesh=mesh,
        in_specs=(
            P(("wide", "narrow"), None, None),
            P(("wide", "narrow"), None),
            P(("wide", "narrow"), None, None),
            P(("wide", "narrow"), None),
            P(("wide", "narrow")),
            P(None, "wide", "narrow", None),
        ),
        out_specs=(
            P(("wide", "narrow"), None, None),
            P("wide", "narrow", None),
            P(None, "wide", "narrow", None),
        ),
        check_vma=False,
    )
```

```python
import functools

import jax
import jax.numpy as jnp
from jax import lax
from jax.experimental import pallas as pl
from jax.experimental.pallas import tpu as pltpu
from jax.sharding import PartitionSpec as P

SWEEPS = 6
DEPTH = SWEEPS + 1
CX, CZ, NY = 4, 8, 512
XS = 2 * CX
XE = XS + 2 * DEPTH
CELLS = 128
SLOTS = 4
KEYS = 4 * SLOTS + 1

f32 = jnp.float32
BLK = 64


def iota(shape, dim):
    return lax.broadcasted_iota(jnp.int32, shape, dim)


def split3(x):
    hi = x.astype(jnp.bfloat16)
    rest = x - hi.astype(f32)
    mid = rest.astype(jnp.bfloat16)
    low = (rest - mid.astype(f32)).astype(jnp.bfloat16)
    return hi, mid, low


def prev_y(x):
    return jnp.where(iota(x.shape, x.ndim - 1) == 0, 0.0, pltpu.roll(x, 1, x.ndim - 1))


def next_y(x):
    return jnp.where(iota(x.shape, x.ndim - 1) == NY - 1, 0.0, pltpu.roll(x, NY - 1, x.ndim - 1))


def split2(x):
    hi = x.astype(jnp.bfloat16).astype(f32)
    return hi, (x - hi).astype(jnp.bfloat16).astype(f32)


def block_products(left, kernel_ref, out, transposed):
    dims = (((1,), (1 if transposed else 0,)), ((), ()))
    hi, low = split2(left)
    for g in range(left.shape[0] // 8):
        rows = slice(8 * g, 8 * g + 8)
        both = jnp.concatenate([hi[rows], low[rows]], axis=0).astype(jnp.bfloat16)
        right = kernel_ref[2 * g : 2 * g + 2].reshape(2 * BLK, CELLS)
        right_hi = right.astype(jnp.bfloat16)
        right_low = (right - right_hi.astype(f32)).astype(jnp.bfloat16)
        first = lax.dot_general(both, right_hi, dims, preferred_element_type=f32)
        second = lax.dot_general(both, right_low, dims, preferred_element_type=f32)
        out[rows, :] = first[0:8] + (first[8:16] + second[0:8])


def slot_codes(brick):
    blocks = brick.shape[1]
    rows, lanes = iota((blocks, blocks), 0), iota((blocks, blocks), 1)
    mine = jnp.broadcast_to(brick.astype(f32), (blocks, blocks))
    other = jnp.sum(jnp.where(rows == lanes, mine, 0.0), axis=1, keepdims=True)
    earlier = jnp.where((other == mine) & (rows < lanes), 1.0, 0.0)
    position = jnp.sum(earlier, axis=0, keepdims=True).astype(jnp.int32)
    return (2 * (brick & 1) + position), brick >> 1


def pack_kernel(brick_ref, tile_ref, volume_ref, velocity_ref, kernel_ref, send_ref, left, sums):
    blocks = volume_ref.shape[0]
    chips = send_ref.shape[0] // KEYS
    slots = chips * SLOTS
    odd = (iota((blocks, BLK), 0) & 1) == 1
    volume = volume_ref[...]
    for k in range(4):
        value = volume if k == 0 else volume * velocity_ref[k - 1]
        left[pl.ds(k, blocks, stride=4), :] = jnp.concatenate(
            [jnp.where(odd, 0.0, value), jnp.where(odd, value, 0.0)], axis=1
        )
    block_products(left[...], kernel_ref, sums, False)
    slot, chip = slot_codes(brick_ref[...])
    code = slot * chips + chip
    match = iota((slots, blocks), 0) == jnp.broadcast_to(code, (slots, blocks))
    move = match.astype(f32).astype(jnp.bfloat16)
    for k in range(4):
        total = jnp.zeros((slots, CELLS), f32)
        for part in split3(sums[pl.ds(k, blocks, stride=4), :]):
            total += jnp.dot(move, part, preferred_element_type=f32)
        for j in range(SLOTS):
            send_ref[pl.ds(j * 4 + k, chips, stride=KEYS), :] = total[
                j * chips : (j + 1) * chips, :
            ]
    tile = jnp.broadcast_to(tile_ref[...].astype(f32), (slots, blocks))
    keys = jnp.sum(jnp.where(match, tile, 0.0), axis=1, keepdims=True)
    lane = iota((chips, CELLS), 1)
    row = jnp.zeros((chips, CELLS), f32)
    for j in range(SLOTS):
        row = jnp.where(lane == j, keys[j * chips : (j + 1) * chips], row)
    send_ref[pl.ds(4 * SLOTS, chips, stride=KEYS), :] = row


def picking(tiles, pick_ref):
    chips = tiles.shape[0]
    tiles = tiles.astype(jnp.int32)
    rows = (tiles >> 5) * 32 + (tiles & 3) * 8 + ((tiles >> 2) & 7)
    cells = iota((chips, XS * 32), 1)
    for j in range(SLOTS):
        mine = rows[:, j : j + 1] + (j // 2) * 128
        pick_ref[pl.ds(j * chips, chips), :] = (cells == mine).astype(f32)


def spread_kernel(recv_ref, fluid_ref, out_ref, pick_ref):
    chips = recv_ref.shape[0] // KEYS
    tiles = recv_ref[pl.ds(4 * SLOTS, chips, stride=KEYS), :]
    picking(tiles, pick_ref)
    for q in range(chips // CZ):
        out_ref[4 * XS + 3 * CX, :, q * CELLS : (q + 1) * CELLS] = tiles[q * CZ : (q + 1) * CZ]
    pick = pick_ref[...].astype(jnp.bfloat16)
    for k in range(4):
        sums = jnp.concatenate(
            [recv_ref[pl.ds(j * 4 + k, chips, stride=KEYS), :] for j in range(SLOTS)], axis=0
        )
        total = jnp.zeros((XS * 32, CELLS), f32)
        for part in split3(sums):
            total += lax.dot_general(
                pick, part, (((0,), (0,)), ((), ())), preferred_element_type=f32
            )
        for x in range(XS):
            for q in range(4):
                out_ref[k * XS + x, :, q * 128 : (q + 1) * 128] = total[
                    x * 32 + q * 8 : x * 32 + q * 8 + 8, :
                ]
    out_ref[4 * XS : 4 * XS + 3 * CX] = fluid_ref[...].reshape(3 * CX, CZ, NY)


ROWS_S = XE - 2
MSG_X = DEPTH + (DEPTH - 1) + 3
PACK_V = (((1, 0), (5, 6)), ((2, 0), (4, 5)), ((3, 0), (6, 4)))
PACK_S = (((1, 0), (3, 5)), ((2, 0), (4, 4), (5, 6)))
MSG_Z = 2 * XS + 2 * (len(PACK_V) + len(PACK_S)) + 3
FACES_Z = MSG_Z - 3


def place(x, start, to, count):
    line = iota(x.shape, 0)
    shift = (to - start) % CZ
    moved = pltpu.roll(x, shift, 0) if shift else x
    return jnp.where((line >= to) & (line < to + count), moved, 0.0)


def packed_rows():
    tile = 2 * XS
    for plan, reach in ((PACK_V, DEPTH), (PACK_S, DEPTH - 1)):
        for side in range(2):
            for group in plan:
                yield tile, reach, [
                    (DEPTH - d if side == 0 else DEPTH + XS - 1 + d, line, reach - d)
                    for d, line in group
                ]
                tile += 1


def fields_kernel(core_ref, own_ref, other_ref, field_ref, aux_ref, send_ref, vx, vz):
    core = core_ref[0]
    z = iota((CZ, NY), 0)
    aux_ref[4 * XS] = own_ref[4 * XS + 3 * CX]
    for x in range(XS):
        sums = [own_ref[k * XS + x] + other_ref[k * XS + x] for k in range(4)]
        mine = core == x // CX
        fluid = [
            jnp.where(
                mine, own_ref[4 * XS + a * CX + x % CX], other_ref[4 * XS + a * CX + x % CX]
            )
            for a in range(3)
        ]
        solid = sums[0]
        growth = (1.0 + solid) ** 2
        void = 1.0 / (1.0 + solid)
        scale = 1.0 / (1.0 + growth * solid)
        provisional = [(fluid[a] + growth * sums[1 + a]) * scale for a in range(3)]
        field_ref[x] = void
        for a in range(3):
            aux_ref[a * XS + x] = provisional[a]
        aux_ref[3 * XS + x] = growth
        vx[x] = void * provisional[0]
        vz[x] = void * provisional[1]
        along_z = vz[x]
        along_y = void * provisional[2]
        field_ref[XS + x] = -0.5 * (
            jnp.where(z == CZ - 1, 0.0, pltpu.roll(along_z, CZ - 1, 0))
            - jnp.where(z == 0, 0.0, pltpu.roll(along_z, 1, 0))
            + next_y(along_y)
            - prev_y(along_y)
        )
    for x in range(XS):
        if x == 0:
            along_x = vx[1]
        elif x == XS - 1:
            along_x = -vx[XS - 2]
        else:
            along_x = vx[x + 1] - vx[x - 1]
        field_ref[XS + x] = field_ref[XS + x] - 0.5 * along_x
        field_ref[2 * XS + 2, x : x + 1, :] = vz[x, 0:1, :]
        field_ref[2 * XS + 3, x : x + 1, :] = vz[x, CZ - 1 : CZ, :]
    field_ref[2 * XS] = vx[0]
    field_ref[2 * XS + 1] = vx[XS - 1]

    def fill(where):
        for d in range(1, DEPTH + 1):
            send_ref[d - 1] = field_ref[where(d)]
        for d in range(1, DEPTH):
            send_ref[DEPTH + d - 1] = field_ref[XS + where(d)]
        send_ref[2 * DEPTH - 1] = vx[where(1)]
        for f in range(2):
            tile = 2 * DEPTH + f
            send_ref[tile] = jnp.zeros((CZ, NY), f32)
            for d in range(1, DEPTH):
                x = where(d)
                send_ref[tile, d - 1 : d, :] = field_ref[2 * XS + 2 + f, x : x + 1, :]

    @pl.when(core == 0)
    def _():
        fill(lambda d: XS - d)

    @pl.when(core != 0)
    def _():
        fill(lambda d: d - 1)


def source_kernel(core_ref, field_ref, recv_ref, swap_ref, send_ref, face_ref, v, s):
    core = core_ref[0]

    def bring(low, high):
        for d in range(1, DEPTH + 1):
            v[DEPTH - d] = low[d - 1]
            v[DEPTH + XS - 1 + d] = high[d - 1]
        for x in range(XS):
            v[DEPTH + x] = field_ref[x]
            s[DEPTH + x] = field_ref[XS + x]
        for d in range(1, DEPTH):
            s[DEPTH - d] = low[DEPTH + d - 1]
            s[DEPTH + XS - 1 + d] = high[DEPTH + d - 1]
        edge = 2 * DEPTH - 1
        s[DEPTH - 1] = s[DEPTH - 1] - 0.5 * field_ref[2 * XS]
        s[DEPTH] = s[DEPTH] + 0.5 * low[edge]
        s[DEPTH + XS - 1] = s[DEPTH + XS - 1] - 0.5 * high[edge]
        s[DEPTH + XS] = s[DEPTH + XS] + 0.5 * field_ref[2 * XS + 1]
        for f in range(2):
            face_ref[3 * f + 2] = jnp.zeros((CZ, NY), f32)
            for i in range(ROWS_S):
                r = i + 1
                if r < DEPTH:
                    d = DEPTH - r
                    value = low[2 * DEPTH + f, d - 1 : d, :]
                elif r < DEPTH + XS:
                    x = r - DEPTH
                    value = field_ref[2 * XS + 2 + f, x : x + 1, :]
                else:
                    d = r - DEPTH - XS + 1
                    value = high[2 * DEPTH + f, d - 1 : d, :]
                face_ref[3 * f + i // 8, i % 8 : i % 8 + 1, :] = value

    @pl.when(core == 0)
    def _():
        bring(recv_ref, swap_ref)

    @pl.when(core != 0)
    def _():
        bring(swap_ref, recv_ref)

    for x in range(XS):
        send_ref[x] = v[DEPTH + x]
        send_ref[XS + x] = s[DEPTH + x]

    def fill(up):
        for tile, reach, rows in packed_rows():
            ref = v if reach == DEPTH else s
            total = None
            for r, line, count in rows:
                part = place(ref[r], CZ - count if up else 0, line, count)
                total = part if total is None else total + part
            send_ref[tile] = total
        for t in range(3):
            send_ref[FACES_Z + t] = face_ref[(3 if up else 0) + t]

    @pl.when(core == 0)
    def _():
        fill(True)

    @pl.when(core != 0)
    def _():
        fill(False)


ZE = 3 * CZ
Q = NY // CELLS
PAD = 8


def solve_kernel(
    core_ref, v_ref, s_ref, face_ref, recv_ref, swap_ref, aux_ref,
    pressure_ref, next_ref, send_ref,
    v, s, xp, xm, zp, zm, yp, ym, pa, pb, faces, coupled, keep, pick_ref,
):
    core = core_ref[0]
    lane = iota((CZ, CELLS), 1)
    sub = iota((CZ, CELLS), 0)

    def at(r, q, z=0):
        return pl.ds((r * Q + q) * ZE + PAD + z, CZ)

    def lanes(q):
        return slice(q * CELLS, (q + 1) * CELLS)

    def bring(low, high):
        none = jnp.zeros((CZ, CELLS), f32)
        for q in range(Q):
            for r in (0, XE - 1):
                v[at(r, q)] = none
                v[at(r, q, 2 * CZ)] = none
            for r in (1, XE - 2):
                s[at(r - 1, q)] = none
                s[at(r - 1, q, 2 * CZ)] = none
            for r in range(XE):
                v[at(r, q, CZ)] = v_ref[r, :, lanes(q)]
            for i in range(ROWS_S):
                s[at(i, q, CZ)] = s_ref[i + 1, :, lanes(q)]
            for x in range(XS):
                v[at(DEPTH + x, q)] = low[x, :, lanes(q)]
                v[at(DEPTH + x, q, 2 * CZ)] = high[x, :, lanes(q)]
                s[at(DEPTH + x - 1, q)] = low[XS + x, :, lanes(q)]
                s[at(DEPTH + x - 1, q, 2 * CZ)] = high[XS + x, :, lanes(q)]
            for tile, reach, rows in packed_rows():
                a, b = low[tile, :, lanes(q)], high[tile, :, lanes(q)]
                for r, line, count in rows:
                    ref, i = (v, r) if reach == DEPTH else (s, r - 1)
                    ref[at(i, q)] = place(a, line, CZ - count, count)
                    ref[at(i, q, 2 * CZ)] = place(b, line, 0, count)
        for f, (ref, base) in enumerate(
            ((face_ref, 0), (face_ref, 3), (low, FACES_Z), (high, FACES_Z))
        ):
            for t in range(3):
                for q in range(Q):
                    faces[(f * Q + q) * 24 + t * 8 : (f * Q + q) * 24 + t * 8 + 8] = ref[
                        base + t, :, lanes(q)
                    ]

    @pl.when(core == 0)
    def _():
        bring(recv_ref, swap_ref)

    @pl.when(core != 0)
    def _():
        bring(swap_ref, recv_ref)

    def shifted(values):
        up = [pltpu.roll(x, CELLS - 1, 1) for x in values]
        down = [pltpu.roll(x, 1, 1) for x in values]
        ups = [jnp.where(lane == CELLS - 1, up[q + 1], up[q]) for q in range(Q - 1)] + [up[-1]]
        downs = [down[0]] + [jnp.where(lane == 0, down[q - 1], down[q]) for q in range(1, Q)]
        return ups, downs

    def weights(r, _):
        i = r - 1

        def face(f, q):
            return jnp.broadcast_to(faces[pl.ds((f * Q + q) * 24 + i, 1)], (CZ, CELLS))

        for z in range(0, ZE, CZ):
            c = [v[at(r, q, z)] for q in range(Q)]
            ups, downs = shifted(c)
            for q in range(Q):
                up, down = ups[q], downs[q]
                if q == Q - 1:
                    up = jnp.where(lane == CELLS - 1, 0.0, up)
                if q == 0:
                    down = jnp.where(lane == 0, 0.0, down)
                here = at(r, q, z)
                t = [
                    c[q] + v[at(r + 1, q, z)],
                    c[q] + v[at(r - 1, q, z)],
                    c[q] + v[at(r, q, z + 1)],
                    c[q] + v[at(r, q, z - 1)],
                    c[q] + up,
                    c[q] + down,
                ]
                total = ((t[0] + t[1]) + (t[2] + t[3])) + (t[4] + t[5])
                some = c[q] > 0.0
                scale = jnp.where(some, 1.0 / jnp.where(some, total, 1.0), 0.0)
                if q == Q - 1:
                    t[4] = jnp.where(lane == CELLS - 1, 0.0, t[4])
                if q == 0:
                    t[5] = jnp.where(lane == 0, 0.0, t[5])
                for ref, value in zip((xp, xm, zp, zm, yp, ym), t):
                    ref[here] = value * scale
                value = s[at(i, q, z)]
                if z == 0:
                    value = value - jnp.where(sub == CZ - 1, 0.5 * face(0, q), 0.0)
                elif z == CZ:
                    value = value + jnp.where(sub == 0, 0.5 * face(2, q), 0.0)
                    value = value - jnp.where(sub == CZ - 1, 0.5 * face(3, q), 0.0)
                else:
                    value = value + jnp.where(sub == 0, 0.5 * face(1, q), 0.0)
                value = (2.0 * value) * scale
                s[at(i, q, z)] = value
                pa[here] = value
        return 0

    for r in range(1, XE - 1):
        weights(r, 0)

    def sweep(src, dst, reach):
        def body(r, _):
            for z in range(0, ZE, CZ):
                p = [src[at(r, q, z)] for q in range(Q)]
                ups, downs = shifted(p)
                for q in range(Q):
                    here = at(r, q, z)
                    a = xp[here] * src[at(r + 1, q, z)] + xm[here] * src[at(r - 1, q, z)]
                    b = zp[here] * src[at(r, q, z + 1)] + zm[here] * src[at(r, q, z - 1)]
                    c = yp[here] * ups[q] + ym[here] * downs[q]
                    dst[here] = (s[at(r - 1, q, z)] + a) + (b + c)
            return 0

        for r in range(DEPTH - reach, DEPTH + XS + reach):
            body(r, 0)

    src, dst = pa, pb
    for k in range(1, SWEEPS):
        sweep(src, dst, SWEEPS - k)
        src, dst = dst, src

    for i in range(CX):
        for q in range(Q):
            pressure_ref[i, :, lanes(q)] = src[at(DEPTH + core * CX + i, q, CZ)]
    for x in range(XS):
        r = DEPTH + x
        p = [src[at(r, q, CZ)] for q in range(Q)]
        ups, downs = shifted(p)
        ups[-1] = jnp.where(lane == CELLS - 1, 0.0, ups[-1])
        downs[0] = jnp.where(lane == 0, 0.0, downs[0])
        for q in range(Q):
            growth = aux_ref[3 * XS + x, :, lanes(q)]
            diffs = [
                src[at(r + 1, q, CZ)] - src[at(r - 1, q, CZ)],
                src[at(r, q, CZ + 1)] - src[at(r, q, CZ - 1)],
                ups[q] - downs[q],
            ]
            put = slice(x * 32 + q * 8, x * 32 + q * 8 + 8)
            for a in range(3):
                value = aux_ref[a * XS + x, :, lanes(q)] - 0.5 * diffs[a]
                coupled[put, lanes(a)] = growth * value
                keep[a * XS + x, :, lanes(q)] = value
            coupled[put, lanes(3)] = growth
    for a in range(3):
        next_ref[a] = keep[pl.ds(a * XS + core * CX, CX)]

    chips = pick_ref.shape[0] // SLOTS
    tiles = aux_ref[4 * XS]
    picking(jnp.concatenate([tiles[:, lanes(q)] for q in range(chips // CZ)], axis=0), pick_ref)
    pick = pick_ref[...].astype(jnp.bfloat16)
    for k in range(4):
        total = jnp.zeros((pick.shape[0], CELLS), f32)
        for part in split3(coupled[:, lanes(k)]):
            total += jnp.dot(pick, part, preferred_element_type=f32)
        for j in range(SLOTS):
            send_ref[pl.ds(j * 4 + k, chips, stride=4 * SLOTS), :] = total[
                j * chips : (j + 1) * chips, :
            ]


def drag_kernel(brick_ref, volume_ref, velocity_ref, kernel_ref, back_ref, drag_ref, left, out):
    blocks = volume_ref.shape[0]
    slots = back_ref.shape[0] // 4
    slot, chip = slot_codes(brick_ref[...])
    code = chip * SLOTS + slot
    match = iota((slots, blocks), 0) == jnp.broadcast_to(code, (slots, blocks))
    move = match.astype(f32).astype(jnp.bfloat16)
    for k in range(4):
        total = jnp.zeros((blocks, CELLS), f32)
        for part in split3(back_ref[pl.ds(k, slots, stride=4), :]):
            total += lax.dot_general(
                move, part, (((0,), (0,)), ((), ())), preferred_element_type=f32
            )
        left[pl.ds(k, blocks, stride=4), :] = total
    block_products(left[...], kernel_ref, out, True)
    odd = (iota((blocks, BLK), 0) & 1) == 1
    sampled = []
    for k in range(4):
        value = out[pl.ds(k, blocks, stride=4), :]
        sampled.append(jnp.where(odd, value[:, BLK:], value[:, :BLK]))
    volume = volume_ref[...]
    for k in range(3):
        drag_ref[k] = volume * sampled[k] - (volume * velocity_ref[k]) * sampled[3]


VMEM = pl.BlockSpec(memory_space=pltpu.VMEM)
SMEM = pl.BlockSpec(memory_space=pltpu.SMEM)


def call(kernel, ins, outs, *args, scratch=(), name=None, grant=4):
    return pl.pallas_call(
        kernel,
        out_shape=[shape for shape, _ in outs],
        in_specs=ins,
        out_specs=[spec for _, spec in outs],
        scratch_shapes=scratch,
        name=name,
        compiler_params=pltpu.CompilerParams(vmem_limit_bytes=grant * 1024 * 1024),
    )(*args)


def arr(*shape):
    return jax.ShapeDtypeStruct(shape, f32)


def local(n_wide, n_narrow, kernel, volume, velocity, block_brick, block_tile, fluid_velocity):
    blocks = kernel.shape[0]
    chips = n_wide // 2
    swap = [(w, w ^ 1) for w in range(n_wide)]
    along_wide = [(w, w + 2) for w in range(0, n_wide - 2, 2)] + [
        (w, w - 2) for w in range(3, n_wide, 2)
    ]
    along_narrow = [
        (w * n_narrow + n, w * n_narrow + t)
        for w in range(n_wide)
        for n in range(n_narrow)
        for t in (n + 1 - 2 * (w % 2),)
        if 0 <= t < n_narrow
    ]
    groups = [list(range(c, n_wide, 2)) for c in range(2)]

    def exchange(x):
        return lax.all_to_all(
            x, "wide", split_axis=0, concat_axis=0, tiled=True, axis_index_groups=groups
        )

    core = (lax.axis_index("wide") % 2).astype(jnp.int32).reshape(1)
    brick = block_brick.reshape(1, blocks)
    by_component = jnp.transpose(velocity, (1, 0, 2))
    (send,) = call(
        pack_kernel,
        [VMEM] * 5,
        [(arr(chips * KEYS, CELLS), VMEM)],
        brick,
        block_tile.reshape(1, blocks),
        volume,
        by_component,
        kernel,
        scratch=[pltpu.VMEM((4 * blocks, CELLS), f32)] * 2,
        name="pack",
    )
    recv = exchange(send.reshape(chips * KEYS, 1, CELLS)).reshape(chips * KEYS, CELLS)
    (part,) = call(
        spread_kernel,
        [VMEM, VMEM],
        [(arr(4 * XS + 3 * CX + 1, CZ, NY), VMEM)],
        recv,
        fluid_velocity,
        scratch=[pltpu.VMEM((SLOTS * chips, XS * 32), f32)],
        name="spread",
    )
    other = lax.ppermute(part, "wide", swap)
    fields, aux, send_x = call(
        fields_kernel,
        [SMEM, VMEM, VMEM],
        [
            (arr(2 * XS + 4, CZ, NY), VMEM),
            (arr(4 * XS + 1, CZ, NY), VMEM),
            (arr(MSG_X, CZ, NY), VMEM),
        ],
        core,
        part,
        other,
        scratch=[pltpu.VMEM((XS, CZ, NY), f32)] * 2,
        name="fields",
    )
    recv_x = lax.ppermute(send_x, "wide", along_wide)
    swap_x = lax.ppermute(recv_x, "wide", swap)
    send_z, faces, void, source = call(
        source_kernel,
        [SMEM, VMEM, VMEM, VMEM],
        [
            (arr(MSG_Z, CZ, NY), VMEM),
            (arr(6, CZ, NY), VMEM),
            (arr(XE, CZ, NY), VMEM),
            (arr(XE - 1, CZ, NY), VMEM),
        ],
        core,
        fields,
        recv_x,
        swap_x,
        name="source",
    )
    recv_z = lax.ppermute(send_z, ("wide", "narrow"), along_narrow)
    swap_z = lax.ppermute(recv_z, "wide", swap)
    region = pltpu.VMEM((XE * Q * ZE + 2 * PAD, CELLS), f32)
    pressure, fluid_next, send_back = call(
        solve_kernel,
        [SMEM] + [VMEM] * 6,
        [
            (arr(CX, CZ, NY), VMEM),
            (arr(3, CX, CZ, NY), VMEM),
            (arr(chips * 4 * SLOTS, CELLS), VMEM),
        ],
        core,
        void,
        source,
        faces,
        recv_z,
        swap_z,
        aux,
        scratch=[region] * 10
        + [
            pltpu.VMEM((4 * Q * 24 + PAD, CELLS), f32),
            pltpu.VMEM((XS * 32, 4 * CELLS), f32),
            pltpu.VMEM((3 * XS, CZ, NY), f32),
            pltpu.VMEM((SLOTS * chips, XS * 32), f32),
        ],
        name="solve",
        grant=16,
    )
    back = exchange(send_back.reshape(chips, 4 * SLOTS, CELLS)).reshape(chips * 4 * SLOTS, CELLS)
    (drag,) = call(
        drag_kernel,
        [VMEM] * 5,
        [(arr(3, blocks, BLK), VMEM)],
        brick,
        volume,
        by_component,
        kernel,
        back,
        scratch=[pltpu.VMEM((4 * blocks, CELLS), f32)] * 2,
        name="drag",
    )
    particle_drag = jnp.transpose(drag, (1, 0, 2))
    return (particle_drag, pressure, fluid_next)


def solution(mesh):
    return jax.shard_map(
        functools.partial(local, mesh.shape["wide"], mesh.shape["narrow"]),
        mesh=mesh,
        in_specs=(
            P(("wide", "narrow"), None, None),
            P(("wide", "narrow"), None),
            P(("wide", "narrow"), None, None),
            P(("wide", "narrow"), None),
            P(("wide", "narrow")),
            P(None, "wide", "narrow", None),
        ),
        out_specs=(
            P(("wide", "narrow"), None, None),
            P("wide", "narrow", None),
            P(None, "wide", "narrow", None),
        ),
        check_vma=False,
    )
```

```python
import functools

import jax
import jax.numpy as jnp
from jax import lax
from jax.experimental import pallas as pl
from jax.experimental.pallas import tpu as pltpu
from jax.sharding import PartitionSpec as P

SWEEPS = 6
DEPTH = SWEEPS + 1
CX, CZ, NY = 4, 8, 512
XS = 2 * CX
XE = XS + 2 * DEPTH
CELLS = 128
SLOTS = 4
KEYS = 4 * SLOTS + 1

f32 = jnp.float32
BLK = 64


def iota(shape, dim):
    return lax.broadcasted_iota(jnp.int32, shape, dim)


def split3(x):
    hi = x.astype(jnp.bfloat16)
    rest = x - hi.astype(f32)
    mid = rest.astype(jnp.bfloat16)
    low = (rest - mid.astype(f32)).astype(jnp.bfloat16)
    return hi, mid, low


def prev_y(x):
    return jnp.where(iota(x.shape, x.ndim - 1) == 0, 0.0, pltpu.roll(x, 1, x.ndim - 1))


def next_y(x):
    return jnp.where(iota(x.shape, x.ndim - 1) == NY - 1, 0.0, pltpu.roll(x, NY - 1, x.ndim - 1))


def split2(x):
    hi = x.astype(jnp.bfloat16).astype(f32)
    return hi, (x - hi).astype(jnp.bfloat16).astype(f32)


def block_products(left, kernel_ref, out, transposed, ready=None):
    dims = (((1,), (1 if transposed else 0,)), ((), ()))
    hi, low = split2(left)
    for g in range(left.shape[0] // 8):
        if ready is not None:
            ready(g)
        rows = slice(8 * g, 8 * g + 8)
        both = jnp.concatenate([hi[rows], low[rows]], axis=0).astype(jnp.bfloat16)
        right = kernel_ref[2 * g : 2 * g + 2].reshape(2 * BLK, CELLS)
        right_hi = right.astype(jnp.bfloat16)
        right_low = (right - right_hi.astype(f32)).astype(jnp.bfloat16)
        first = lax.dot_general(both, right_hi, dims, preferred_element_type=f32)
        second = lax.dot_general(both, right_low, dims, preferred_element_type=f32)
        out[rows, :] = first[0:8] + (first[8:16] + second[0:8])


def slot_codes(brick):
    blocks = brick.shape[1]
    rows, lanes = iota((blocks, blocks), 0), iota((blocks, blocks), 1)
    mine = jnp.broadcast_to(brick.astype(f32), (blocks, blocks))
    other = jnp.sum(jnp.where(rows == lanes, mine, 0.0), axis=1, keepdims=True)
    earlier = jnp.where((other == mine) & (rows < lanes), 1.0, 0.0)
    position = jnp.sum(earlier, axis=0, keepdims=True).astype(jnp.int32)
    return (2 * (brick & 1) + position), brick >> 1


PIECES = 4


def pack_kernel(
    brick_hbm, tile_hbm, volume_hbm, velocity_hbm, kernel_hbm,
    send_ref,
    brick_ref, tile_ref, volume_ref, velocity_ref, kernel_ref, left, sums, sem,
):
    blocks = volume_ref.shape[0]
    chips = send_ref.shape[0] // KEYS
    slots = chips * SLOTS
    piece = blocks // PIECES
    small = [
        pltpu.make_async_copy(src, dst, sem.at[i])
        for i, (src, dst) in enumerate(
            (
                (volume_hbm, volume_ref),
                (velocity_hbm, velocity_ref),
                (brick_hbm, brick_ref),
                (tile_hbm, tile_ref),
            )
        )
    ]
    large = [
        pltpu.make_async_copy(
            kernel_hbm.at[pl.ds(i * piece, piece)],
            kernel_ref.at[pl.ds(i * piece, piece)],
            sem.at[len(small) + i],
        )
        for i in range(PIECES)
    ]
    for copy in small + large:
        copy.start()

    def ready(g):
        if (2 * g) % piece == 0:
            large[2 * g // piece].wait()

    for copy in small:
        copy.wait()
    slot, chip = slot_codes(brick_ref[...])
    code = slot * chips + chip
    match = iota((slots, blocks), 0) == jnp.broadcast_to(code, (slots, blocks))
    tile = jnp.broadcast_to(tile_ref[...].astype(f32), (slots, blocks))
    keys = jnp.sum(jnp.where(match, tile, 0.0), axis=1, keepdims=True)
    lane = iota((chips, CELLS), 1)
    row = jnp.zeros((chips, CELLS), f32)
    for j in range(SLOTS):
        row = jnp.where(lane == j, keys[j * chips : (j + 1) * chips], row)
    send_ref[pl.ds(4 * SLOTS, chips, stride=KEYS), :] = row
    odd = (iota((blocks, BLK), 0) & 1) == 1
    volume = volume_ref[...]
    for k in range(4):
        value = volume if k == 0 else volume * velocity_ref[k - 1]
        left[pl.ds(k, blocks, stride=4), :] = jnp.concatenate(
            [jnp.where(odd, 0.0, value), jnp.where(odd, value, 0.0)], axis=1
        )
    block_products(left[...], kernel_ref, sums, False, ready)
    move = match.astype(f32).astype(jnp.bfloat16)
    for k in range(4):
        total = jnp.zeros((slots, CELLS), f32)
        for part in split3(sums[pl.ds(k, blocks, stride=4), :]):
            total += jnp.dot(move, part, preferred_element_type=f32)
        for j in range(SLOTS):
            send_ref[pl.ds(j * 4 + k, chips, stride=KEYS), :] = total[
                j * chips : (j + 1) * chips, :
            ]


def picking(tiles, pick_ref):
    chips = tiles.shape[0]
    tiles = tiles.astype(jnp.int32)
    rows = (tiles >> 5) * 32 + (tiles & 3) * 8 + ((tiles >> 2) & 7)
    cells = iota((chips, XS * 32), 1)
    for j in range(SLOTS):
        mine = rows[:, j : j + 1] + (j // 2) * 128
        pick_ref[pl.ds(j * chips, chips), :] = (cells == mine).astype(f32)


def spread_kernel(recv_ref, fluid_ref, out_ref, pick_ref):
    chips = recv_ref.shape[0] // KEYS
    tiles = recv_ref[pl.ds(4 * SLOTS, chips, stride=KEYS), :]
    picking(tiles, pick_ref)
    for q in range(chips // CZ):
        out_ref[4 * XS + 3 * CX, :, q * CELLS : (q + 1) * CELLS] = tiles[q * CZ : (q + 1) * CZ]
    pick = pick_ref[...].astype(jnp.bfloat16)
    for k in range(4):
        sums = jnp.concatenate(
            [recv_ref[pl.ds(j * 4 + k, chips, stride=KEYS), :] for j in range(SLOTS)], axis=0
        )
        total = jnp.zeros((XS * 32, CELLS), f32)
        for part in split3(sums):
            total += lax.dot_general(
                pick, part, (((0,), (0,)), ((), ())), preferred_element_type=f32
            )
        for x in range(XS):
            for q in range(4):
                out_ref[k * XS + x, :, q * 128 : (q + 1) * 128] = total[
                    x * 32 + q * 8 : x * 32 + q * 8 + 8, :
                ]
    out_ref[4 * XS : 4 * XS + 3 * CX] = fluid_ref[...].reshape(3 * CX, CZ, NY)


ROWS_S = XE - 2
MSG_X = DEPTH + (DEPTH - 1) + 3
PACK_V = (((1, 0), (5, 6)), ((2, 0), (4, 5)), ((3, 0), (6, 4)))
PACK_S = (((1, 0), (3, 5)), ((2, 0), (4, 4), (5, 6)))
MSG_Z = 2 * XS + 2 * (len(PACK_V) + len(PACK_S)) + 3
FACES_Z = MSG_Z - 3


def place(x, start, to, count):
    line = iota(x.shape, 0)
    shift = (to - start) % CZ
    moved = pltpu.roll(x, shift, 0) if shift else x
    return jnp.where((line >= to) & (line < to + count), moved, 0.0)


def packed_rows():
    tile = 2 * XS
    for plan, reach in ((PACK_V, DEPTH), (PACK_S, DEPTH - 1)):
        for side in range(2):
            for group in plan:
                yield tile, reach, [
                    (DEPTH - d if side == 0 else DEPTH + XS - 1 + d, line, reach - d)
                    for d, line in group
                ]
                tile += 1


def fields_kernel(core_ref, own_ref, other_ref, field_ref, aux_ref, send_ref, vx, vz):
    core = core_ref[0]
    z = iota((CZ, NY), 0)
    aux_ref[4 * XS] = own_ref[4 * XS + 3 * CX]
    for x in range(XS):
        sums = [own_ref[k * XS + x] + other_ref[k * XS + x] for k in range(4)]
        mine = core == x // CX
        fluid = [
            jnp.where(
                mine, own_ref[4 * XS + a * CX + x % CX], other_ref[4 * XS + a * CX + x % CX]
            )
            for a in range(3)
        ]
        solid = sums[0]
        growth = (1.0 + solid) ** 2
        void = 1.0 / (1.0 + solid)
        scale = 1.0 / (1.0 + growth * solid)
        provisional = [(fluid[a] + growth * sums[1 + a]) * scale for a in range(3)]
        field_ref[x] = void
        for a in range(3):
            aux_ref[a * XS + x] = provisional[a]
        aux_ref[3 * XS + x] = growth
        vx[x] = void * provisional[0]
        vz[x] = void * provisional[1]
        along_z = vz[x]
        along_y = void * provisional[2]
        field_ref[XS + x] = -0.5 * (
            jnp.where(z == CZ - 1, 0.0, pltpu.roll(along_z, CZ - 1, 0))
            - jnp.where(z == 0, 0.0, pltpu.roll(along_z, 1, 0))
            + next_y(along_y)
            - prev_y(along_y)
        )
    for x in range(XS):
        if x == 0:
            along_x = vx[1]
        elif x == XS - 1:
            along_x = -vx[XS - 2]
        else:
            along_x = vx[x + 1] - vx[x - 1]
        field_ref[XS + x] = field_ref[XS + x] - 0.5 * along_x
        field_ref[2 * XS + 2, x : x + 1, :] = vz[x, 0:1, :]
        field_ref[2 * XS + 3, x : x + 1, :] = vz[x, CZ - 1 : CZ, :]
    field_ref[2 * XS] = vx[0]
    field_ref[2 * XS + 1] = vx[XS - 1]

    def fill(where):
        for d in range(1, DEPTH + 1):
            send_ref[d - 1] = field_ref[where(d)]
        for d in range(1, DEPTH):
            send_ref[DEPTH + d - 1] = field_ref[XS + where(d)]
        send_ref[2 * DEPTH - 1] = vx[where(1)]
        for f in range(2):
            tile = 2 * DEPTH + f
            send_ref[tile] = jnp.zeros((CZ, NY), f32)
            for d in range(1, DEPTH):
                x = where(d)
                send_ref[tile, d - 1 : d, :] = field_ref[2 * XS + 2 + f, x : x + 1, :]

    @pl.when(core == 0)
    def _():
        fill(lambda d: XS - d)

    @pl.when(core != 0)
    def _():
        fill(lambda d: d - 1)


def source_kernel(core_ref, field_ref, recv_ref, swap_ref, send_ref, face_ref, v, s):
    core = core_ref[0]

    def bring(low, high):
        for d in range(1, DEPTH + 1):
            v[DEPTH - d] = low[d - 1]
            v[DEPTH + XS - 1 + d] = high[d - 1]
        for x in range(XS):
            v[DEPTH + x] = field_ref[x]
            s[DEPTH + x] = field_ref[XS + x]
        for d in range(1, DEPTH):
            s[DEPTH - d] = low[DEPTH + d - 1]
            s[DEPTH + XS - 1 + d] = high[DEPTH + d - 1]
        edge = 2 * DEPTH - 1
        s[DEPTH - 1] = s[DEPTH - 1] - 0.5 * field_ref[2 * XS]
        s[DEPTH] = s[DEPTH] + 0.5 * low[edge]
        s[DEPTH + XS - 1] = s[DEPTH + XS - 1] - 0.5 * high[edge]
        s[DEPTH + XS] = s[DEPTH + XS] + 0.5 * field_ref[2 * XS + 1]
        for f in range(2):
            face_ref[3 * f + 2] = jnp.zeros((CZ, NY), f32)
            for i in range(ROWS_S):
                r = i + 1
                if r < DEPTH:
                    d = DEPTH - r
                    value = low[2 * DEPTH + f, d - 1 : d, :]
                elif r < DEPTH + XS:
                    x = r - DEPTH
                    value = field_ref[2 * XS + 2 + f, x : x + 1, :]
                else:
                    d = r - DEPTH - XS + 1
                    value = high[2 * DEPTH + f, d - 1 : d, :]
                face_ref[3 * f + i // 8, i % 8 : i % 8 + 1, :] = value

    @pl.when(core == 0)
    def _():
        bring(recv_ref, swap_ref)

    @pl.when(core != 0)
    def _():
        bring(swap_ref, recv_ref)

    for x in range(XS):
        send_ref[x] = v[DEPTH + x]
        send_ref[XS + x] = s[DEPTH + x]

    def fill(up):
        for tile, reach, rows in packed_rows():
            ref = v if reach == DEPTH else s
            total = None
            for r, line, count in rows:
                part = place(ref[r], CZ - count if up else 0, line, count)
                total = part if total is None else total + part
            send_ref[tile] = total
        for t in range(3):
            send_ref[FACES_Z + t] = face_ref[(3 if up else 0) + t]

    @pl.when(core == 0)
    def _():
        fill(True)

    @pl.when(core != 0)
    def _():
        fill(False)


ZE = 3 * CZ
Q = NY // CELLS
PAD = 8


def solve_kernel(
    core_ref, v_ref, s_ref, face_ref, recv_ref, swap_ref, aux_ref,
    pressure_ref, next_ref, send_ref,
    v, s, xp, xm, zp, zm, yp, ym, pa, pb, faces, coupled, keep, pick_ref, press, sem,
):
    core = core_ref[0]
    lane = iota((CZ, CELLS), 1)
    sub = iota((CZ, CELLS), 0)

    def at(r, q, z=0):
        return pl.ds((r * Q + q) * ZE + PAD + z, CZ)

    def lanes(q):
        return slice(q * CELLS, (q + 1) * CELLS)

    def bring(low, high):
        none = jnp.zeros((CZ, CELLS), f32)
        for q in range(Q):
            for r in (0, XE - 1):
                v[at(r, q)] = none
                v[at(r, q, 2 * CZ)] = none
            for r in (1, XE - 2):
                s[at(r - 1, q)] = none
                s[at(r - 1, q, 2 * CZ)] = none
            for r in range(XE):
                v[at(r, q, CZ)] = v_ref[r, :, lanes(q)]
            for i in range(ROWS_S):
                s[at(i, q, CZ)] = s_ref[i + 1, :, lanes(q)]
            for x in range(XS):
                v[at(DEPTH + x, q)] = low[x, :, lanes(q)]
                v[at(DEPTH + x, q, 2 * CZ)] = high[x, :, lanes(q)]
                s[at(DEPTH + x - 1, q)] = low[XS + x, :, lanes(q)]
                s[at(DEPTH + x - 1, q, 2 * CZ)] = high[XS + x, :, lanes(q)]
            for tile, reach, rows in packed_rows():
                a, b = low[tile, :, lanes(q)], high[tile, :, lanes(q)]
                for r, line, count in rows:
                    ref, i = (v, r) if reach == DEPTH else (s, r - 1)
                    ref[at(i, q)] = place(a, line, CZ - count, count)
                    ref[at(i, q, 2 * CZ)] = place(b, line, 0, count)
        for f, (ref, base) in enumerate(
            ((face_ref, 0), (face_ref, 3), (low, FACES_Z), (high, FACES_Z))
        ):
            for t in range(3):
                for q in range(Q):
                    faces[(f * Q + q) * 24 + t * 8 : (f * Q + q) * 24 + t * 8 + 8] = ref[
                        base + t, :, lanes(q)
                    ]

    @pl.when(core == 0)
    def _():
        bring(recv_ref, swap_ref)

    @pl.when(core != 0)
    def _():
        bring(swap_ref, recv_ref)

    def shifted(values):
        up = [pltpu.roll(x, CELLS - 1, 1) for x in values]
        down = [pltpu.roll(x, 1, 1) for x in values]
        ups = [jnp.where(lane == CELLS - 1, up[q + 1], up[q]) for q in range(Q - 1)] + [up[-1]]
        downs = [down[0]] + [jnp.where(lane == 0, down[q - 1], down[q]) for q in range(1, Q)]
        return ups, downs

    def weights(r, _):
        i = r - 1

        def face(f, q):
            return jnp.broadcast_to(faces[pl.ds((f * Q + q) * 24 + i, 1)], (CZ, CELLS))

        for z in range(0, ZE, CZ):
            c = [v[at(r, q, z)] for q in range(Q)]
            ups, downs = shifted(c)
            for q in range(Q):
                up, down = ups[q], downs[q]
                if q == Q - 1:
                    up = jnp.where(lane == CELLS - 1, 0.0, up)
                if q == 0:
                    down = jnp.where(lane == 0, 0.0, down)
                here = at(r, q, z)
                t = [
                    c[q] + v[at(r + 1, q, z)],
                    c[q] + v[at(r - 1, q, z)],
                    c[q] + v[at(r, q, z + 1)],
                    c[q] + v[at(r, q, z - 1)],
                    c[q] + up,
                    c[q] + down,
                ]
                total = ((t[0] + t[1]) + (t[2] + t[3])) + (t[4] + t[5])
                some = c[q] > 0.0
                scale = jnp.where(some, 1.0 / jnp.where(some, total, 1.0), 0.0)
                if q == Q - 1:
                    t[4] = jnp.where(lane == CELLS - 1, 0.0, t[4])
                if q == 0:
                    t[5] = jnp.where(lane == 0, 0.0, t[5])
                for ref, value in zip((xp, xm, zp, zm, yp, ym), t):
                    ref[here] = value * scale
                value = s[at(i, q, z)]
                if z == 0:
                    value = value - jnp.where(sub == CZ - 1, 0.5 * face(0, q), 0.0)
                elif z == CZ:
                    value = value + jnp.where(sub == 0, 0.5 * face(2, q), 0.0)
                    value = value - jnp.where(sub == CZ - 1, 0.5 * face(3, q), 0.0)
                else:
                    value = value + jnp.where(sub == 0, 0.5 * face(1, q), 0.0)
                value = (2.0 * value) * scale
                s[at(i, q, z)] = value
                pa[here] = value
        return 0

    for r in range(1, XE - 1):
        weights(r, 0)

    def sweep(src, dst, reach):
        def body(r, _):
            for z in range(0, ZE, CZ):
                p = [src[at(r, q, z)] for q in range(Q)]
                ups, downs = shifted(p)
                for q in range(Q):
                    here = at(r, q, z)
                    a = xp[here] * src[at(r + 1, q, z)] + xm[here] * src[at(r - 1, q, z)]
                    b = zp[here] * src[at(r, q, z + 1)] + zm[here] * src[at(r, q, z - 1)]
                    c = yp[here] * ups[q] + ym[here] * downs[q]
                    dst[here] = (s[at(r - 1, q, z)] + a) + (b + c)
            return 0

        for r in range(DEPTH - reach, DEPTH + XS + reach):
            body(r, 0)

    src, dst = pa, pb
    for k in range(1, SWEEPS):
        sweep(src, dst, SWEEPS - k)
        src, dst = dst, src

    for i in range(CX):
        for q in range(Q):
            press[i, :, lanes(q)] = src[at(DEPTH + core * CX + i, q, CZ)]
    copies = [pltpu.make_async_copy(press, pressure_ref, sem.at[3])]
    copies[0].start()
    for x in range(XS):
        r = DEPTH + x
        p = [src[at(r, q, CZ)] for q in range(Q)]
        ups, downs = shifted(p)
        ups[-1] = jnp.where(lane == CELLS - 1, 0.0, ups[-1])
        downs[0] = jnp.where(lane == 0, 0.0, downs[0])
        for q in range(Q):
            growth = aux_ref[3 * XS + x, :, lanes(q)]
            diffs = [
                src[at(r + 1, q, CZ)] - src[at(r - 1, q, CZ)],
                src[at(r, q, CZ + 1)] - src[at(r, q, CZ - 1)],
                ups[q] - downs[q],
            ]
            put = slice(x * 32 + q * 8, x * 32 + q * 8 + 8)
            for a in range(3):
                value = aux_ref[a * XS + x, :, lanes(q)] - 0.5 * diffs[a]
                coupled[put, lanes(a)] = growth * value
                keep[a * XS + x, :, lanes(q)] = value
            coupled[put, lanes(3)] = growth
    for a in range(3):
        copies.append(
            pltpu.make_async_copy(keep.at[pl.ds(a * XS + core * CX, CX)], next_ref.at[a], sem.at[a])
        )
        copies[-1].start()

    chips = pick_ref.shape[0] // SLOTS
    tiles = aux_ref[4 * XS]
    picking(jnp.concatenate([tiles[:, lanes(q)] for q in range(chips // CZ)], axis=0), pick_ref)
    pick = pick_ref[...].astype(jnp.bfloat16)
    for k in range(4):
        total = jnp.zeros((pick.shape[0], CELLS), f32)
        for part in split3(coupled[:, lanes(k)]):
            total += jnp.dot(pick, part, preferred_element_type=f32)
        for j in range(SLOTS):
            send_ref[pl.ds(j * 4 + k, chips, stride=4 * SLOTS), :] = total[
                j * chips : (j + 1) * chips, :
            ]
    for copy in copies:
        copy.wait()


def drag_kernel(brick_ref, volume_ref, velocity_ref, kernel_ref, back_ref, drag_ref, left, out):
    blocks = volume_ref.shape[0]
    slots = back_ref.shape[0] // 4
    slot, chip = slot_codes(brick_ref[...])
    code = chip * SLOTS + slot
    match = iota((slots, blocks), 0) == jnp.broadcast_to(code, (slots, blocks))
    move = match.astype(f32).astype(jnp.bfloat16)
    for k in range(4):
        total = jnp.zeros((blocks, CELLS), f32)
        for part in split3(back_ref[pl.ds(k, slots, stride=4), :]):
            total += lax.dot_general(
                move, part, (((0,), (0,)), ((), ())), preferred_element_type=f32
            )
        left[pl.ds(k, blocks, stride=4), :] = total
    block_products(left[...], kernel_ref, out, True)
    odd = (iota((blocks, BLK), 0) & 1) == 1
    sampled = []
    for k in range(4):
        value = out[pl.ds(k, blocks, stride=4), :]
        sampled.append(jnp.where(odd, value[:, BLK:], value[:, :BLK]))
    volume = volume_ref[...]
    for k in range(3):
        drag_ref[k] = volume * sampled[k] - (volume * velocity_ref[k]) * sampled[3]


VMEM = pl.BlockSpec(memory_space=pltpu.VMEM)
SMEM = pl.BlockSpec(memory_space=pltpu.SMEM)
HBM = pl.BlockSpec(memory_space=pltpu.HBM)


def call(kernel, ins, outs, *args, scratch=(), name=None, grant=4):
    return pl.pallas_call(
        kernel,
        out_shape=[shape for shape, _ in outs],
        in_specs=ins,
        out_specs=[spec for _, spec in outs],
        scratch_shapes=scratch,
        name=name,
        compiler_params=pltpu.CompilerParams(vmem_limit_bytes=grant * 1024 * 1024),
    )(*args)


def arr(*shape):
    return jax.ShapeDtypeStruct(shape, f32)


def local(n_wide, n_narrow, kernel, volume, velocity, block_brick, block_tile, fluid_velocity):
    blocks = kernel.shape[0]
    chips = n_wide // 2
    swap = [(w, w ^ 1) for w in range(n_wide)]
    along_wide = [(w, w + 2) for w in range(0, n_wide - 2, 2)] + [
        (w, w - 2) for w in range(3, n_wide, 2)
    ]
    along_narrow = [
        (w * n_narrow + n, w * n_narrow + t)
        for w in range(n_wide)
        for n in range(n_narrow)
        for t in (n + 1 - 2 * (w % 2),)
        if 0 <= t < n_narrow
    ]
    groups = [list(range(c, n_wide, 2)) for c in range(2)]

    def exchange(x):
        return lax.all_to_all(
            x, "wide", split_axis=0, concat_axis=0, tiled=True, axis_index_groups=groups
        )

    core = (lax.axis_index("wide") % 2).astype(jnp.int32).reshape(1)
    brick = block_brick.reshape(1, blocks)
    by_component = jnp.transpose(velocity, (1, 0, 2))
    (send,) = call(
        pack_kernel,
        [HBM] * 5,
        [(arr(chips * KEYS, CELLS), VMEM)],
        brick,
        block_tile.reshape(1, blocks),
        volume,
        by_component,
        kernel,
        scratch=[
            pltpu.VMEM((1, blocks), jnp.int32),
            pltpu.VMEM((1, blocks), jnp.int32),
            pltpu.VMEM((blocks, BLK), f32),
            pltpu.VMEM((3, blocks, BLK), f32),
            pltpu.VMEM((blocks, BLK, CELLS), f32),
            pltpu.VMEM((4 * blocks, CELLS), f32),
            pltpu.VMEM((4 * blocks, CELLS), f32),
            pltpu.SemaphoreType.DMA((4 + PIECES,)),
        ],
        grant=60,
        name="pack",
    )
    recv = exchange(send.reshape(chips * KEYS, 1, CELLS)).reshape(chips * KEYS, CELLS)
    (part,) = call(
        spread_kernel,
        [VMEM, VMEM],
        [(arr(4 * XS + 3 * CX + 1, CZ, NY), VMEM)],
        recv,
        fluid_velocity,
        scratch=[pltpu.VMEM((SLOTS * chips, XS * 32), f32)],
        name="spread",
    )
    other = lax.ppermute(part, "wide", swap)
    fields, aux, send_x = call(
        fields_kernel,
        [SMEM, VMEM, VMEM],
        [
            (arr(2 * XS + 4, CZ, NY), VMEM),
            (arr(4 * XS + 1, CZ, NY), VMEM),
            (arr(MSG_X, CZ, NY), VMEM),
        ],
        core,
        part,
        other,
        scratch=[pltpu.VMEM((XS, CZ, NY), f32)] * 2,
        name="fields",
    )
    recv_x = lax.ppermute(send_x, "wide", along_wide)
    swap_x = lax.ppermute(recv_x, "wide", swap)
    send_z, faces, void, source = call(
        source_kernel,
        [SMEM, VMEM, VMEM, VMEM],
        [
            (arr(MSG_Z, CZ, NY), VMEM),
            (arr(6, CZ, NY), VMEM),
            (arr(XE, CZ, NY), VMEM),
            (arr(XE - 1, CZ, NY), VMEM),
        ],
        core,
        fields,
        recv_x,
        swap_x,
        name="source",
    )
    recv_z = lax.ppermute(send_z, ("wide", "narrow"), along_narrow)
    swap_z = lax.ppermute(recv_z, "wide", swap)
    region = pltpu.VMEM((XE * Q * ZE + 2 * PAD, CELLS), f32)
    pressure, fluid_next, send_back = call(
        solve_kernel,
        [SMEM] + [VMEM] * 6,
        [
            (arr(CX, CZ, NY), HBM),
            (arr(3, CX, CZ, NY), HBM),
            (arr(chips * 4 * SLOTS, CELLS), VMEM),
        ],
        core,
        void,
        source,
        faces,
        recv_z,
        swap_z,
        aux,
        scratch=[region] * 10
        + [
            pltpu.VMEM((4 * Q * 24 + PAD, CELLS), f32),
            pltpu.VMEM((XS * 32, 4 * CELLS), f32),
            pltpu.VMEM((3 * XS, CZ, NY), f32),
            pltpu.VMEM((SLOTS * chips, XS * 32), f32),
            pltpu.VMEM((CX, CZ, NY), f32),
            pltpu.SemaphoreType.DMA((4,)),
        ],
        name="solve",
        grant=16,
    )
    back = exchange(send_back.reshape(chips, 4 * SLOTS, CELLS)).reshape(chips * 4 * SLOTS, CELLS)
    (drag,) = call(
        drag_kernel,
        [VMEM] * 5,
        [(arr(3, blocks, BLK), VMEM)],
        brick,
        volume,
        by_component,
        kernel,
        back,
        scratch=[pltpu.VMEM((4 * blocks, CELLS), f32)] * 2,
        name="drag",
    )
    particle_drag = jnp.transpose(drag, (1, 0, 2))
    return (particle_drag, pressure, fluid_next)


def solution(mesh):
    return jax.shard_map(
        functools.partial(local, mesh.shape["wide"], mesh.shape["narrow"]),
        mesh=mesh,
        in_specs=(
            P(("wide", "narrow"), None, None),
            P(("wide", "narrow"), None),
            P(("wide", "narrow"), None, None),
            P(("wide", "narrow"), None),
            P(("wide", "narrow")),
            P(None, "wide", "narrow", None),
        ),
        out_specs=(
            P(("wide", "narrow"), None, None),
            P("wide", "narrow", None),
            P(None, "wide", "narrow", None),
        ),
        check_vma=False,
    )
```

```python
import functools

import jax
import jax.numpy as jnp
from jax import lax
from jax.experimental import pallas as pl
from jax.experimental.pallas import tpu as pltpu
from jax.sharding import PartitionSpec as P

SWEEPS = 6
DEPTH = SWEEPS + 1
CX, CZ, NY = 4, 8, 512
XS = 2 * CX
XE = XS + 2 * DEPTH
CELLS = 128
SLOTS = 4
KEYS = 4 * SLOTS + 1

f32 = jnp.float32
BLK = 64


def iota(shape, dim):
    return lax.broadcasted_iota(jnp.int32, shape, dim)


def split3(x):
    hi = x.astype(jnp.bfloat16)
    rest = x - hi.astype(f32)
    mid = rest.astype(jnp.bfloat16)
    low = (rest - mid.astype(f32)).astype(jnp.bfloat16)
    return hi, mid, low


def prev_y(x):
    return jnp.where(iota(x.shape, x.ndim - 1) == 0, 0.0, pltpu.roll(x, 1, x.ndim - 1))


def next_y(x):
    return jnp.where(iota(x.shape, x.ndim - 1) == NY - 1, 0.0, pltpu.roll(x, NY - 1, x.ndim - 1))


def split2(x):
    hi = x.astype(jnp.bfloat16).astype(f32)
    return hi, (x - hi).astype(jnp.bfloat16).astype(f32)


def block_products(left, kernel_ref, out, transposed, ready=None):
    dims = (((1,), (1 if transposed else 0,)), ((), ()))
    hi, low = split2(left)
    for g in range(left.shape[0] // 8):
        if ready is not None:
            ready(g)
        rows = slice(8 * g, 8 * g + 8)
        both = jnp.concatenate([hi[rows], low[rows]], axis=0).astype(jnp.bfloat16)
        right = kernel_ref[2 * g : 2 * g + 2].reshape(2 * BLK, CELLS)
        right_hi = right.astype(jnp.bfloat16)
        right_low = (right - right_hi.astype(f32)).astype(jnp.bfloat16)
        first = lax.dot_general(both, right_hi, dims, preferred_element_type=f32)
        second = lax.dot_general(both, right_low, dims, preferred_element_type=f32)
        out[rows, :] = first[0:8] + (first[8:16] + second[0:8])


def slot_codes(brick):
    blocks = brick.shape[1]
    rows, lanes = iota((blocks, blocks), 0), iota((blocks, blocks), 1)
    mine = jnp.broadcast_to(brick.astype(f32), (blocks, blocks))
    other = jnp.sum(jnp.where(rows == lanes, mine, 0.0), axis=1, keepdims=True)
    earlier = jnp.where((other == mine) & (rows < lanes), 1.0, 0.0)
    position = jnp.sum(earlier, axis=0, keepdims=True).astype(jnp.int32)
    return (2 * (brick & 1) + position), brick >> 1


PIECES = 4


def pack_kernel(
    brick_hbm, tile_hbm, volume_hbm, velocity_hbm, kernel_hbm,
    send_ref,
    brick_ref, tile_ref, volume_ref, velocity_ref, kernel_ref, left, sums, sem,
):
    blocks = volume_ref.shape[0]
    chips = send_ref.shape[0] // KEYS
    slots = chips * SLOTS
    piece = blocks // PIECES
    small = [
        pltpu.make_async_copy(src, dst, sem.at[i])
        for i, (src, dst) in enumerate(
            (
                (volume_hbm, volume_ref),
                (velocity_hbm, velocity_ref),
                (brick_hbm, brick_ref),
                (tile_hbm, tile_ref),
            )
        )
    ]
    large = [
        pltpu.make_async_copy(
            kernel_hbm.at[pl.ds(i * piece, piece)],
            kernel_ref.at[pl.ds(i * piece, piece)],
            sem.at[len(small) + i],
        )
        for i in range(PIECES)
    ]
    for copy in small + large:
        copy.start()

    def ready(g):
        if (2 * g) % piece == 0:
            large[2 * g // piece].wait()

    for copy in small:
        copy.wait()
    slot, chip = slot_codes(brick_ref[...])
    code = slot * chips + chip
    match = iota((slots, blocks), 0) == jnp.broadcast_to(code, (slots, blocks))
    tile = jnp.broadcast_to(tile_ref[...].astype(f32), (slots, blocks))
    keys = jnp.sum(jnp.where(match, tile, 0.0), axis=1, keepdims=True)
    lane = iota((chips, CELLS), 1)
    row = jnp.zeros((chips, CELLS), f32)
    for j in range(SLOTS):
        row = jnp.where(lane == j, keys[j * chips : (j + 1) * chips], row)
    send_ref[pl.ds(4 * SLOTS, chips, stride=KEYS), :] = row
    odd = (iota((blocks, BLK), 0) & 1) == 1
    volume = volume_ref[...]
    for k in range(4):
        value = volume if k == 0 else volume * velocity_ref[k - 1]
        left[pl.ds(k, blocks, stride=4), :] = jnp.concatenate(
            [jnp.where(odd, 0.0, value), jnp.where(odd, value, 0.0)], axis=1
        )
    block_products(left[...], kernel_ref, sums, False, ready)
    move = match.astype(f32).astype(jnp.bfloat16)
    for k in range(4):
        total = jnp.zeros((slots, CELLS), f32)
        for part in split3(sums[pl.ds(k, blocks, stride=4), :]):
            total += jnp.dot(move, part, preferred_element_type=f32)
        for j in range(SLOTS):
            send_ref[pl.ds(j * 4 + k, chips, stride=KEYS), :] = total[
                j * chips : (j + 1) * chips, :
            ]


def picking(tiles, pick_ref):
    chips = tiles.shape[0]
    tiles = tiles.astype(jnp.int32)
    rows = (tiles >> 5) * 32 + (tiles & 3) * 8 + ((tiles >> 2) & 7)
    cells = iota((chips, XS * 32), 1)
    for j in range(SLOTS):
        mine = rows[:, j : j + 1] + (j // 2) * 128
        pick_ref[pl.ds(j * chips, chips), :] = (cells == mine).astype(f32)


def spread_kernel(recv_ref, fluid_ref, out_ref, pick_ref):
    chips = recv_ref.shape[0] // KEYS
    tiles = recv_ref[pl.ds(4 * SLOTS, chips, stride=KEYS), :]
    picking(tiles, pick_ref)
    for q in range(chips // CZ):
        out_ref[4 * XS + 3 * CX, :, q * CELLS : (q + 1) * CELLS] = tiles[q * CZ : (q + 1) * CZ]
    pick = pick_ref[...].astype(jnp.bfloat16)
    for k in range(4):
        sums = jnp.concatenate(
            [recv_ref[pl.ds(j * 4 + k, chips, stride=KEYS), :] for j in range(SLOTS)], axis=0
        )
        total = jnp.zeros((XS * 32, CELLS), f32)
        for part in split3(sums):
            total += lax.dot_general(
                pick, part, (((0,), (0,)), ((), ())), preferred_element_type=f32
            )
        for x in range(XS):
            for q in range(4):
                out_ref[k * XS + x, :, q * 128 : (q + 1) * 128] = total[
                    x * 32 + q * 8 : x * 32 + q * 8 + 8, :
                ]
    out_ref[4 * XS : 4 * XS + 3 * CX] = fluid_ref[...].reshape(3 * CX, CZ, NY)


ROWS_S = XE - 2
MSG_X = DEPTH + (DEPTH - 1) + 3
PACK_V = (((1, 0), (5, 6)), ((2, 0), (4, 5)), ((3, 0), (6, 4)))
PACK_S = (((1, 0), (3, 5)), ((2, 0), (4, 4), (5, 6)))
HALF = 2 * CX + len(PACK_V) + len(PACK_S) + 2
FACES_Z = HALF - 2
LINES = ROWS_S // 2


def place(x, start, to, count):
    line = iota(x.shape, 0)
    shift = (to - start) % CZ
    moved = pltpu.roll(x, shift, 0) if shift else x
    return jnp.where((line >= to) & (line < to + count), moved, 0.0)


def packed_rows():
    tile = 2 * CX
    for plan, reach in ((PACK_V, DEPTH), (PACK_S, DEPTH - 1)):
        for group in plan:
            yield tile, reach, [(d, line, reach - d) for d, line in group]
            tile += 1


def fields_kernel(core_ref, own_ref, other_ref, field_ref, aux_ref, send_ref, vx, vz):
    core = core_ref[0]
    z = iota((CZ, NY), 0)
    aux_ref[4 * XS] = own_ref[4 * XS + 3 * CX]
    for x in range(XS):
        sums = [own_ref[k * XS + x] + other_ref[k * XS + x] for k in range(4)]
        mine = core == x // CX
        fluid = [
            jnp.where(
                mine, own_ref[4 * XS + a * CX + x % CX], other_ref[4 * XS + a * CX + x % CX]
            )
            for a in range(3)
        ]
        solid = sums[0]
        growth = (1.0 + solid) ** 2
        void = 1.0 / (1.0 + solid)
        scale = 1.0 / (1.0 + growth * solid)
        provisional = [(fluid[a] + growth * sums[1 + a]) * scale for a in range(3)]
        field_ref[x] = void
        for a in range(3):
            aux_ref[a * XS + x] = provisional[a]
        aux_ref[3 * XS + x] = growth
        vx[x] = void * provisional[0]
        vz[x] = void * provisional[1]
        along_z = vz[x]
        along_y = void * provisional[2]
        field_ref[XS + x] = -0.5 * (
            jnp.where(z == CZ - 1, 0.0, pltpu.roll(along_z, CZ - 1, 0))
            - jnp.where(z == 0, 0.0, pltpu.roll(along_z, 1, 0))
            + next_y(along_y)
            - prev_y(along_y)
        )
    for x in range(XS):
        if x == 0:
            along_x = vx[1]
        elif x == XS - 1:
            along_x = -vx[XS - 2]
        else:
            along_x = vx[x + 1] - vx[x - 1]
        field_ref[XS + x] = field_ref[XS + x] - 0.5 * along_x
        field_ref[2 * XS + 2, x : x + 1, :] = vz[x, 0:1, :]
        field_ref[2 * XS + 3, x : x + 1, :] = vz[x, CZ - 1 : CZ, :]
    field_ref[2 * XS] = vx[0]
    field_ref[2 * XS + 1] = vx[XS - 1]

    def fill(where):
        for d in range(1, DEPTH + 1):
            send_ref[d - 1] = field_ref[where(d)]
        for d in range(1, DEPTH):
            send_ref[DEPTH + d - 1] = field_ref[XS + where(d)]
        send_ref[2 * DEPTH - 1] = vx[where(1)]
        for f in range(2):
            tile = 2 * DEPTH + f
            send_ref[tile] = jnp.zeros((CZ, NY), f32)
            for d in range(1, DEPTH):
                x = where(d)
                send_ref[tile, d - 1 : d, :] = field_ref[2 * XS + 2 + f, x : x + 1, :]

    @pl.when(core == 0)
    def _():
        fill(lambda d: XS - d)

    @pl.when(core != 0)
    def _():
        fill(lambda d: d - 1)


EDGE = 2 * DEPTH - 1


def half_kernel(core_ref, field_ref, recv_ref, up_ref, down_ref):
    core = core_ref[0]

    def fill(half):
        def source(d):
            value = recv_ref[DEPTH + d - 1]
            if d == 1:
                value = value + (0.5 if half else -0.5) * field_ref[2 * XS + half]
            return value

        for i in range(CX):
            x = half * CX + i
            value = field_ref[XS + x]
            if x == 0:
                value = value + 0.5 * recv_ref[EDGE]
            if x == XS - 1:
                value = value - 0.5 * recv_ref[EDGE]
            for ref in (up_ref, down_ref):
                ref[i] = field_ref[x]
                ref[CX + i] = value
        for tile, reach, rows in packed_rows():
            up = down = None
            for d, line, count in rows:
                value = recv_ref[d - 1] if reach == DEPTH else source(d)
                one, two = place(value, CZ - count, line, count), place(value, 0, line, count)
                up, down = (one, two) if up is None else (up + one, down + two)
            up_ref[tile] = up
            down_ref[tile] = down
        for f, ref in enumerate((down_ref, up_ref)):
            ref[FACES_Z + 1] = jnp.zeros((CZ, NY), f32)
            for line in range(LINES):
                r = 1 + half * LINES + line
                if DEPTH <= r < DEPTH + XS:
                    x = r - DEPTH
                    value = field_ref[2 * XS + 2 + f, x : x + 1, :]
                else:
                    d = r - DEPTH - XS + 1 if half else DEPTH - r
                    value = recv_ref[2 * DEPTH + f, d - 1 : d, :]
                ref[FACES_Z + line // 8, line % 8 : line % 8 + 1, :] = value

    @pl.when(core == 0)
    def _():
        fill(0)

    @pl.when(core != 0)
    def _():
        fill(1)


def source_kernel(
    core_ref, field_ref, recv_ref, swap_ref, low_ref, high_ref, send_ref, face_ref, v, s
):
    core = core_ref[0]
    send_ref[0:HALF] = low_ref[...]
    send_ref[HALF:] = high_ref[...]

    def bring(low, high):
        for d in range(1, DEPTH + 1):
            v[DEPTH - d] = low[d - 1]
            v[DEPTH + XS - 1 + d] = high[d - 1]
        for x in range(XS):
            v[DEPTH + x] = field_ref[x]
            s[DEPTH + x] = field_ref[XS + x]
        for d in range(1, DEPTH):
            s[DEPTH - d] = low[DEPTH + d - 1]
            s[DEPTH + XS - 1 + d] = high[DEPTH + d - 1]
        edge = 2 * DEPTH - 1
        s[DEPTH - 1] = s[DEPTH - 1] - 0.5 * field_ref[2 * XS]
        s[DEPTH] = s[DEPTH] + 0.5 * low[edge]
        s[DEPTH + XS - 1] = s[DEPTH + XS - 1] - 0.5 * high[edge]
        s[DEPTH + XS] = s[DEPTH + XS] + 0.5 * field_ref[2 * XS + 1]
        for f in range(2):
            face_ref[3 * f + 2] = jnp.zeros((CZ, NY), f32)
            for i in range(ROWS_S):
                r = i + 1
                if r < DEPTH:
                    d = DEPTH - r
                    value = low[2 * DEPTH + f, d - 1 : d, :]
                elif r < DEPTH + XS:
                    x = r - DEPTH
                    value = field_ref[2 * XS + 2 + f, x : x + 1, :]
                else:
                    d = r - DEPTH - XS + 1
                    value = high[2 * DEPTH + f, d - 1 : d, :]
                face_ref[3 * f + i // 8, i % 8 : i % 8 + 1, :] = value

    @pl.when(core == 0)
    def _():
        bring(recv_ref, swap_ref)

    @pl.when(core != 0)
    def _():
        bring(swap_ref, recv_ref)


ZE = 3 * CZ
Q = NY // CELLS
PAD = 8


def solve_kernel(
    core_ref, v_ref, s_ref, face_ref, recv_ref, swap_ref, aux_ref,
    pressure_ref, next_ref, send_ref,
    v, s, xp, xm, zp, zm, yp, ym, pa, pb, faces, coupled, keep, pick_ref, press, sem,
):
    core = core_ref[0]
    lane = iota((CZ, CELLS), 1)
    sub = iota((CZ, CELLS), 0)

    def at(r, q, z=0):
        return pl.ds((r * Q + q) * ZE + PAD + z, CZ)

    def lanes(q):
        return slice(q * CELLS, (q + 1) * CELLS)

    def bring(*halves):
        none = jnp.zeros((CZ, CELLS), f32)
        for q in range(Q):
            for r in (0, XE - 1):
                v[at(r, q)] = none
                v[at(r, q, 2 * CZ)] = none
            for r in (1, XE - 2):
                s[at(r - 1, q)] = none
                s[at(r - 1, q, 2 * CZ)] = none
            for r in range(XE):
                v[at(r, q, CZ)] = v_ref[r, :, lanes(q)]
            for i in range(ROWS_S):
                s[at(i, q, CZ)] = s_ref[i + 1, :, lanes(q)]
            for half, ref in enumerate(halves):
                for i in range(CX):
                    r = DEPTH + half * CX + i
                    v[at(r, q)] = ref[i, :, lanes(q)]
                    v[at(r, q, 2 * CZ)] = ref[HALF + i, :, lanes(q)]
                    s[at(r - 1, q)] = ref[CX + i, :, lanes(q)]
                    s[at(r - 1, q, 2 * CZ)] = ref[HALF + CX + i, :, lanes(q)]
                for tile, reach, rows in packed_rows():
                    a, b = ref[tile, :, lanes(q)], ref[HALF + tile, :, lanes(q)]
                    for d, line, count in rows:
                        r = DEPTH + XS - 1 + d if half else DEPTH - d
                        to, i = (v, r) if reach == DEPTH else (s, r - 1)
                        to[at(i, q)] = place(a, line, CZ - count, count)
                        to[at(i, q, 2 * CZ)] = place(b, line, 0, count)
        for q in range(Q):
            for f in range(2):
                for t in range(3):
                    base = (f * Q + q) * 24 + t * 8
                    faces[base : base + 8] = face_ref[3 * f + t, :, lanes(q)]
                for half, ref in enumerate(halves):
                    base = ((2 + f) * Q + q) * 24 + half * LINES
                    tile = f * HALF + FACES_Z
                    faces[base : base + 8] = ref[tile, :, lanes(q)]
                    faces[base + 8 : base + LINES] = ref[tile + 1, 0 : LINES - 8, lanes(q)]

    @pl.when(core == 0)
    def _():
        bring(recv_ref, swap_ref)

    @pl.when(core != 0)
    def _():
        bring(swap_ref, recv_ref)

    def shifted(values):
        up = [pltpu.roll(x, CELLS - 1, 1) for x in values]
        down = [pltpu.roll(x, 1, 1) for x in values]
        ups = [jnp.where(lane == CELLS - 1, up[q + 1], up[q]) for q in range(Q - 1)] + [up[-1]]
        downs = [down[0]] + [jnp.where(lane == 0, down[q - 1], down[q]) for q in range(1, Q)]
        return ups, downs

    def weights(r):
        i = r - 1

        def face(f, q):
            return jnp.broadcast_to(faces[pl.ds((f * Q + q) * 24 + i, 1)], (CZ, CELLS))

        for z in range(0, ZE, CZ):
            c = [v[at(r, q, z)] for q in range(Q)]
            ups, downs = shifted(c)
            for q in range(Q):
                up, down = ups[q], downs[q]
                if q == Q - 1:
                    up = jnp.where(lane == CELLS - 1, 0.0, up)
                if q == 0:
                    down = jnp.where(lane == 0, 0.0, down)
                here = at(r, q, z)
                t = [
                    c[q] + v[at(r + 1, q, z)],
                    c[q] + v[at(r - 1, q, z)],
                    c[q] + v[at(r, q, z + 1)],
                    c[q] + v[at(r, q, z - 1)],
                    c[q] + up,
                    c[q] + down,
                ]
                total = ((t[0] + t[1]) + (t[2] + t[3])) + (t[4] + t[5])
                some = c[q] > 0.0
                scale = jnp.where(some, 1.0 / jnp.where(some, total, 1.0), 0.0)
                if q == Q - 1:
                    t[4] = jnp.where(lane == CELLS - 1, 0.0, t[4])
                if q == 0:
                    t[5] = jnp.where(lane == 0, 0.0, t[5])
                for ref, value in zip((xp, xm, zp, zm, yp, ym), t):
                    ref[here] = value * scale
                value = s[at(i, q, z)]
                if z == 0:
                    value = value - jnp.where(sub == CZ - 1, 0.5 * face(0, q), 0.0)
                elif z == CZ:
                    value = value + jnp.where(sub == 0, 0.5 * face(2, q), 0.0)
                    value = value - jnp.where(sub == CZ - 1, 0.5 * face(3, q), 0.0)
                else:
                    value = value + jnp.where(sub == 0, 0.5 * face(1, q), 0.0)
                value = (2.0 * value) * scale
                s[at(i, q, z)] = value
                pa[here] = value
        return 0

    for r in range(1, XE - 1):
        weights(r)

    def sweep(src, dst, reach):
        def body(r):
            ends = (DEPTH - reach, DEPTH + XS + reach - 1)
            for z in (CZ,) if r in ends else range(0, ZE, CZ):
                p = [src[at(r, q, z)] for q in range(Q)]
                ups, downs = shifted(p)
                for q in range(Q):
                    here = at(r, q, z)
                    a = xp[here] * src[at(r + 1, q, z)] + xm[here] * src[at(r - 1, q, z)]
                    b = zp[here] * src[at(r, q, z + 1)] + zm[here] * src[at(r, q, z - 1)]
                    c = yp[here] * ups[q] + ym[here] * downs[q]
                    dst[here] = (s[at(r - 1, q, z)] + a) + (b + c)
            return 0

        for r in range(DEPTH - reach, DEPTH + XS + reach):
            body(r)

    src, dst = pa, pb
    for k in range(1, SWEEPS):
        sweep(src, dst, SWEEPS - k)
        src, dst = dst, src

    for i in range(CX):
        for q in range(Q):
            press[i, :, lanes(q)] = src[at(DEPTH + core * CX + i, q, CZ)]
    copies = [pltpu.make_async_copy(press, pressure_ref, sem.at[3])]
    copies[0].start()
    for x in range(XS):
        r = DEPTH + x
        p = [src[at(r, q, CZ)] for q in range(Q)]
        ups, downs = shifted(p)
        ups[-1] = jnp.where(lane == CELLS - 1, 0.0, ups[-1])
        downs[0] = jnp.where(lane == 0, 0.0, downs[0])
        for q in range(Q):
            growth = aux_ref[3 * XS + x, :, lanes(q)]
            diffs = [
                src[at(r + 1, q, CZ)] - src[at(r - 1, q, CZ)],
                src[at(r, q, CZ + 1)] - src[at(r, q, CZ - 1)],
                ups[q] - downs[q],
            ]
            put = slice(x * 32 + q * 8, x * 32 + q * 8 + 8)
            for a in range(3):
                value = aux_ref[a * XS + x, :, lanes(q)] - 0.5 * diffs[a]
                coupled[put, lanes(a)] = growth * value
                keep[a * XS + x, :, lanes(q)] = value
            coupled[put, lanes(3)] = growth
    for a in range(3):
        copies.append(
            pltpu.make_async_copy(keep.at[pl.ds(a * XS + core * CX, CX)], next_ref.at[a], sem.at[a])
        )
        copies[-1].start()

    chips = pick_ref.shape[0] // SLOTS
    tiles = aux_ref[4 * XS]
    picking(jnp.concatenate([tiles[:, lanes(q)] for q in range(chips // CZ)], axis=0), pick_ref)
    pick = pick_ref[...].astype(jnp.bfloat16)
    for k in range(4):
        total = jnp.zeros((pick.shape[0], CELLS), f32)
        for part in split3(coupled[:, lanes(k)]):
            total += jnp.dot(pick, part, preferred_element_type=f32)
        for j in range(SLOTS):
            send_ref[pl.ds(j * 4 + k, chips, stride=4 * SLOTS), :] = total[
                j * chips : (j + 1) * chips, :
            ]
    for copy in copies:
        copy.wait()


def drag_kernel(brick_ref, volume_ref, velocity_ref, kernel_ref, back_ref, drag_ref, left, out):
    blocks = volume_ref.shape[0]
    slots = back_ref.shape[0] // 4
    slot, chip = slot_codes(brick_ref[...])
    code = chip * SLOTS + slot
    match = iota((slots, blocks), 0) == jnp.broadcast_to(code, (slots, blocks))
    move = match.astype(f32).astype(jnp.bfloat16)
    for k in range(4):
        total = jnp.zeros((blocks, CELLS), f32)
        for part in split3(back_ref[pl.ds(k, slots, stride=4), :]):
            total += lax.dot_general(
                move, part, (((0,), (0,)), ((), ())), preferred_element_type=f32
            )
        left[pl.ds(k, blocks, stride=4), :] = total
    block_products(left[...], kernel_ref, out, True)
    odd = (iota((blocks, BLK), 0) & 1) == 1
    sampled = []
    for k in range(4):
        value = out[pl.ds(k, blocks, stride=4), :]
        sampled.append(jnp.where(odd, value[:, BLK:], value[:, :BLK]))
    volume = volume_ref[...]
    for k in range(3):
        drag_ref[k] = volume * sampled[k] - (volume * velocity_ref[k]) * sampled[3]


VMEM = pl.BlockSpec(memory_space=pltpu.VMEM)
SMEM = pl.BlockSpec(memory_space=pltpu.SMEM)
HBM = pl.BlockSpec(memory_space=pltpu.HBM)


def call(kernel, ins, outs, *args, scratch=(), grant=4):
    return pl.pallas_call(
        kernel,
        out_shape=[shape for shape, _ in outs],
        in_specs=ins,
        out_specs=[spec for _, spec in outs],
        scratch_shapes=scratch,
        compiler_params=pltpu.CompilerParams(vmem_limit_bytes=grant * 1024 * 1024),
    )(*args)


def arr(*shape):
    return jax.ShapeDtypeStruct(shape, f32)


def local(n_wide, n_narrow, kernel, volume, velocity, block_brick, block_tile, fluid_velocity):
    blocks = kernel.shape[0]
    chips = n_wide // 2
    swap = [(w, w ^ 1) for w in range(n_wide)]
    along_wide = [(w, w + 2) for w in range(0, n_wide - 2, 2)] + [
        (w, w - 2) for w in range(3, n_wide, 2)
    ]
    upward = [(n, n + 1) for n in range(n_narrow - 1)]
    downward = [(t, n) for n, t in upward]
    groups = [list(range(c, n_wide, 2)) for c in range(2)]

    def exchange(x):
        return lax.all_to_all(
            x, "wide", split_axis=0, concat_axis=0, tiled=True, axis_index_groups=groups
        )

    core = (lax.axis_index("wide") % 2).astype(jnp.int32).reshape(1)
    brick = block_brick.reshape(1, blocks)
    by_component = jnp.transpose(velocity, (1, 0, 2))
    (send,) = call(
        pack_kernel,
        [HBM] * 5,
        [(arr(chips * KEYS, CELLS), VMEM)],
        brick,
        block_tile.reshape(1, blocks),
        volume,
        by_component,
        kernel,
        scratch=[
            pltpu.VMEM((1, blocks), jnp.int32),
            pltpu.VMEM((1, blocks), jnp.int32),
            pltpu.VMEM((blocks, BLK), f32),
            pltpu.VMEM((3, blocks, BLK), f32),
            pltpu.VMEM((blocks, BLK, CELLS), f32),
            pltpu.VMEM((4 * blocks, CELLS), f32),
            pltpu.VMEM((4 * blocks, CELLS), f32),
            pltpu.SemaphoreType.DMA((4 + PIECES,)),
        ],
        grant=60,
    )
    recv = exchange(send.reshape(chips * KEYS, 1, CELLS)).reshape(chips * KEYS, CELLS)
    (part,) = call(
        spread_kernel,
        [VMEM, VMEM],
        [(arr(4 * XS + 3 * CX + 1, CZ, NY), VMEM)],
        recv,
        fluid_velocity,
        scratch=[pltpu.VMEM((SLOTS * chips, XS * 32), f32)],
    )
    other = lax.ppermute(part, "wide", swap)
    fields, aux, send_x = call(
        fields_kernel,
        [SMEM, VMEM, VMEM],
        [
            (arr(2 * XS + 4, CZ, NY), VMEM),
            (arr(4 * XS + 1, CZ, NY), VMEM),
            (arr(MSG_X, CZ, NY), VMEM),
        ],
        core,
        part,
        other,
        scratch=[pltpu.VMEM((XS, CZ, NY), f32)] * 2,
    )
    recv_x = lax.ppermute(send_x, "wide", along_wide)
    send_up, send_down = call(
        half_kernel, [SMEM, VMEM, VMEM], [(arr(HALF, CZ, NY), VMEM)] * 2, core, fields, recv_x
    )
    from_low = lax.ppermute(send_up, "narrow", upward)
    from_high = lax.ppermute(send_down, "narrow", downward)
    swap_x = lax.ppermute(recv_x, "wide", swap)
    recv_z, faces, void, source = call(
        source_kernel,
        [SMEM] + [VMEM] * 5,
        [
            (arr(2 * HALF, CZ, NY), VMEM),
            (arr(6, CZ, NY), VMEM),
            (arr(XE, CZ, NY), VMEM),
            (arr(XE - 1, CZ, NY), VMEM),
        ],
        core,
        fields,
        recv_x,
        swap_x,
        from_low,
        from_high,
    )
    swap_z = lax.ppermute(recv_z, "wide", swap)
    region = pltpu.VMEM((XE * Q * ZE + 2 * PAD, CELLS), f32)
    pressure, fluid_next, send_back = call(
        solve_kernel,
        [SMEM] + [VMEM] * 6,
        [
            (arr(CX, CZ, NY), HBM),
            (arr(3, CX, CZ, NY), HBM),
            (arr(chips * 4 * SLOTS, CELLS), VMEM),
        ],
        core,
        void,
        source,
        faces,
        recv_z,
        swap_z,
        aux,
        scratch=[region] * 10
        + [
            pltpu.VMEM((4 * Q * 24 + PAD, CELLS), f32),
            pltpu.VMEM((XS * 32, 4 * CELLS), f32),
            pltpu.VMEM((3 * XS, CZ, NY), f32),
            pltpu.VMEM((SLOTS * chips, XS * 32), f32),
            pltpu.VMEM((CX, CZ, NY), f32),
            pltpu.SemaphoreType.DMA((4,)),
        ],
        grant=16,
    )
    back = exchange(send_back.reshape(chips, 4 * SLOTS, CELLS)).reshape(chips * 4 * SLOTS, CELLS)
    (drag,) = call(
        drag_kernel,
        [VMEM] * 5,
        [(arr(3, blocks, BLK), VMEM)],
        brick,
        volume,
        by_component,
        kernel,
        back,
        scratch=[pltpu.VMEM((4 * blocks, CELLS), f32)] * 2,
    )
    particle_drag = jnp.transpose(drag, (1, 0, 2))
    return (particle_drag, pressure, fluid_next)


def solution(mesh):
    return jax.shard_map(
        functools.partial(local, mesh.shape["wide"], mesh.shape["narrow"]),
        mesh=mesh,
        in_specs=(
            P(("wide", "narrow"), None, None),
            P(("wide", "narrow"), None),
            P(("wide", "narrow"), None, None),
            P(("wide", "narrow"), None),
            P(("wide", "narrow")),
            P(None, "wide", "narrow", None),
        ),
        out_specs=(
            P(("wide", "narrow"), None, None),
            P("wide", "narrow", None),
            P(None, "wide", "narrow", None),
        ),
        check_vma=False,
    )
```
